32 devices in a mesh: groups: 2 (over y), ctx: 8 (over z, x), head: 2 (over core).
Axes of the slice: x: 2, y: 2, z: 4, core: 2. Of those that a mesh axis runs over, the one named last changes fastest.
Arguments:
- queries: bfloat16 [4096, 512], P(('groups', 'ctx'), 'head'), parts along dimension 0, may hold values from -5 to 5
- key_input: bfloat16 [4096, 128], P(('groups', 'ctx')), parts along dimension 0, may hold values from -5 to 5
- value_input: bfloat16 [4096, 128], P(('groups', 'ctx')), parts along dimension 0, may hold values from -2.5 to 2.5
- grad_out: bfloat16 [4096, 512], P(('groups', 'ctx'), 'head'), parts along dimension 0, may hold values from -1.5 to 1.5
- doc_lengths: int32 [32], P('groups'), parts along dimension 0, may hold values from 1 to 512, 2048 in all
- stretch_plan: int32 [32], P(('groups', 'ctx')), parts along dimension 0, may hold values from 0 to 15, as said below
Outputs:
- output: bfloat16 [4096, 512], P(('groups', 'ctx'), 'head'), parts along dimension 0
- query_grad: float32 [4096, 512], P(('groups', 'ctx'), 'head'), parts along dimension 0
- key_grad: float32 [4096, 128], P(('groups', 'ctx')), parts along dimension 0
- value_grad: float32 [4096, 128], P(('groups', 'ctx')), parts along dimension 0
The draws below stay inside these ranges and needn't reach their ends.
There are 2 independent parts, one for each index of `groups`. The reference program is written for one: setup_inputs(seed, part) draws one part's arguments, and reference() takes and returns one part's arrays. A program takes and returns all parts, laid end to end along the dimension named above; each array names one. Nothing has to cross between parts.
Inputs may be any that keep to these rules, and one draw needn't show every extreme that they name: A permutation of the stretch numbers: slot j holds stretch stretch_plan[j], and |stretch_plan[j] - j| <= 4 for every slot, with equality for some slot.
All inputs are finite; a program needn't handle non-finite values.
Results may differ from the reference program's by a relative error of at most 0.025.
Values may be sent and summed in bfloat16 or wider, within the bound.
No kernel may reach another device: no remote copies, remote signals or barrier semaphores. Data moves between devices by JAX's collectives and lax.ppermute only.
A program may use at most 64 MiB of HBM per device.

```python
import math
import jax
import jax.numpy as jnp
import numpy as np
from jax import lax

DH = 128
QHEADS = 4
TOK_DEV = 256
HOPS = 2
TOKENS = 2048
STRETCH = 128
STRETCHES = 16
DOC_MAX = 512
DOCS = 16
N_CTX = 8


def draw_queries(key, part):
    drawn = jax.random.normal(jax.random.fold_in(key, 1), (TOKENS, QHEADS * DH))
    return jnp.clip(drawn, -4.5, 4.5).astype(jnp.bfloat16)


def draw_key_input(key, part):
    drawn = jax.random.normal(jax.random.fold_in(key, 2), (TOKENS, DH))
    return jnp.clip(drawn, -4.5, 4.5).astype(jnp.bfloat16)


def draw_stretch_plan(key, part):
    spread = 2 * HOPS
    numbers = jnp.arange(STRETCHES, dtype=jnp.int32)
    noise = jax.random.randint(jax.random.fold_in(key, 3), (STRETCHES,), 0, spread + 2)
    noise = jnp.where(numbers == 0, spread + 1, jnp.where(numbers <= spread + 1, 0, noise))
    far_end = STRETCHES - 1 - spread
    noise = jnp.where(numbers == far_end, spread + 1, jnp.where(numbers > far_end, 0, noise))
    ranking = (numbers + noise) * STRETCHES + numbers
    return jnp.argsort(ranking).astype(jnp.int32)


def block_levels(own_key, extent, shards, smallest, top_value):
    gain = 1.0
    for axis_at, parts in shards:
        draws = jax.random.uniform(jax.random.fold_in(jax.random.fold_in(own_key, 6), axis_at), (parts,), jnp.float32, smallest / len(shards), top_value / len(shards))
        gain = gain * jnp.repeat(jnp.exp(draws), extent[axis_at] // parts).reshape((-1,) + (1,) * (len(extent) - 1 - axis_at))
    return gain


def length_profile(number_of, total, most, lean):
    portions = [(1 << 20) // math.isqrt(rank ** lean) + 1 for rank in range(2, number_of + 1)]
    rest, given = total - most - (number_of - 1), [1] * (number_of - 1)
    while rest > 0:
        candidates = [i for i in range(number_of - 1) if given[i] < most]
        mass, left = sum([portions[i] for i in candidates]), rest
        for i in candidates:
            extra = min(most - given[i], max(1, left * portions[i] // mass), rest)
            given[i] = given[i] + extra
            rest = rest - extra
    return np.array([most] + given)


def uneven_parts(rng, count, total, bound, lean):
    if count == 2:
        one = jax.random.randint(rng, (), max(1, total - bound), min(bound, total - 1) + 1)
        return jnp.stack([one, total - one])
    tallies = jnp.asarray(length_profile(count, total, bound, lean), jnp.int32)
    couples = (count - 1) // 2
    source_of, sink = tallies[1:1 + 2 * couples:2], tallies[2:2 + 2 * couples:2]
    margin = jnp.minimum(source_of - 1, bound - sink)
    shifted = jax.random.randint(jax.random.fold_in(rng, 1), (couples,), 0, 1 << 20) % (margin + 1)
    tallies = tallies.at[1:1 + 2 * couples:2].set(source_of - shifted).at[2:2 + 2 * couples:2].set(sink + shifted)
    return tallies[jax.random.permutation(jax.random.fold_in(rng, 2), count)]


def gaussian(key, extent, scale, reach, pieces=(), kind=jnp.bfloat16):
    drawn = scale * jax.random.normal(key, extent, jnp.float32)
    if pieces:
        drawn = drawn * block_levels(key, extent, pieces, -0.22, 0.18)
    return jnp.clip(drawn, -reach, reach).astype(kind)


def setup_inputs(seed: int = 0, part: int = 0) -> dict:
    splits = jax.random.split(jax.random.key(seed), 7)
    own_keys = jax.random.split(jax.random.fold_in(splits[6], part), 7)
    queries = draw_queries(jax.random.fold_in(jax.random.fold_in(splits[6], part), 71), part)
    key_input = draw_key_input(jax.random.fold_in(jax.random.fold_in(splits[6], part), 71), part)
    value_input = gaussian(own_keys[2], (TOKENS, DH), 0.5, 2.5, ((0, 8),))
    grad_out = gaussian(own_keys[3], (TOKENS, QHEADS * DH), 0.25, 1.5, ((0, 8), (1, 2)))
    doc_lengths = uneven_parts(own_keys[4], DOCS, TOKENS, DOC_MAX, 2).astype(jnp.int32)
    stretch_plan = draw_stretch_plan(jax.random.fold_in(jax.random.fold_in(splits[6], part), 71), part)
    return dict(queries=queries, key_input=key_input, value_input=value_input, grad_out=grad_out, doc_lengths=doc_lengths, stretch_plan=stretch_plan)


neg_large = -1e+30

def doc_numbers(bounds, places):
    return lax.optimization_barrier(jnp.sum((bounds[None, :] <= places[:, None]).astype(jnp.int32), axis=1))

def rounded(values_f32):
    return lax.optimization_barrier(values_f32.astype(jnp.bfloat16)).astype(jnp.float32)

def reference(queries, key_input, value_input, grad_out, doc_lengths, stretch_plan):
    inv_root = 1.0 / math.sqrt(DH)
    bounds = jnp.cumsum(doc_lengths).astype(jnp.int32)
    places = jnp.arange(TOKENS, dtype=jnp.int32)
    docs = doc_numbers(bounds, places)
    front = DOC_MAX
    key_padded = jnp.concatenate([jnp.zeros((front, DH), jnp.float32), key_input.astype(jnp.float32)], axis=0)
    value_padded = jnp.concatenate([jnp.zeros((front, DH), jnp.float32), value_input.astype(jnp.float32)], axis=0)
    docs_padded = jnp.concatenate([jnp.full((front,), -1, jnp.int32), docs])
    query_heads = queries.reshape(TOKENS, QHEADS, DH)
    grad_heads = grad_out.reshape(TOKENS, QHEADS, DH)
    key_width = front + TOK_DEV

    def one_block(carried, block_number):
        key_total, value_total = carried
        row_start = (block_number * TOK_DEV).astype(jnp.int32)
        query_block = lax.dynamic_slice_in_dim(query_heads, row_start, TOK_DEV, 0).astype(jnp.float32)
        grad_block = lax.dynamic_slice_in_dim(grad_heads, row_start, TOK_DEV, 0).astype(jnp.float32)
        query_places = row_start + jnp.arange(TOK_DEV, dtype=jnp.int32)
        query_docs = lax.dynamic_slice_in_dim(docs, row_start, TOK_DEV, 0)
        key_block = lax.dynamic_slice_in_dim(key_padded, row_start, key_width, 0)
        value_block = lax.dynamic_slice_in_dim(value_padded, row_start, key_width, 0)
        key_docs = lax.dynamic_slice_in_dim(docs_padded, row_start, key_width, 0)
        key_places = row_start - front + jnp.arange(key_width, dtype=jnp.int32)
        allowed = (query_docs[:, None] == key_docs[None, :]) & (key_places[None, :] <= query_places[:, None])
        scores = jnp.einsum('phd,td->pht', query_block, key_block) * inv_root
        scores = jnp.where(allowed[:, None, :], scores, neg_large)
        row_top = lax.optimization_barrier(jnp.max(scores, axis=2))
        row_total = lax.optimization_barrier(jnp.sum(jnp.where(allowed[:, None, :], jnp.exp(scores - row_top[:, :, None]), 0.0), axis=2))
        log_total = row_top + jnp.log(row_total)
        weights = jnp.where(allowed[:, None, :], jnp.exp(scores - log_total[:, :, None]), 0.0)
        weights_b = rounded(weights)
        attended = jnp.einsum('pht,td->phd', weights_b, value_block).astype(jnp.bfloat16)
        row_dots = lax.optimization_barrier(jnp.sum(grad_block * attended.astype(jnp.float32), axis=2))
        grad_weights = jnp.einsum('phd,td->pht', grad_block, value_block)
        grad_scores = rounded(weights * (grad_weights - row_dots[:, :, None]))
        query_nat = jnp.einsum('pht,td->phd', grad_scores, key_block) * inv_root
        key_part = jnp.einsum('pht,phd->td', grad_scores, query_block)
        value_part = jnp.einsum('pht,phd->td', weights_b, grad_block)
        key_total = lax.dynamic_update_slice_in_dim(key_total, lax.dynamic_slice_in_dim(key_total, row_start, key_width, 0) + key_part, row_start, 0)
        value_total = lax.dynamic_update_slice_in_dim(value_total, lax.dynamic_slice_in_dim(value_total, row_start, key_width, 0) + value_part, row_start, 0)
        return ((key_total, value_total), (attended, query_nat))
    zeros_pad = jnp.zeros((TOKENS + front, DH), jnp.float32)
    totals, outputs = lax.scan(one_block, (zeros_pad, zeros_pad), jnp.arange(N_CTX, dtype=jnp.int32))
    key_total, value_total = totals
    attended_all = outputs[0].reshape(STRETCHES, STRETCH, QHEADS * DH)
    query_all = outputs[1].reshape(STRETCHES, STRETCH, QHEADS * DH)
    output = attended_all[stretch_plan].reshape(TOKENS, QHEADS * DH)
    query_grad = query_all[stretch_plan].reshape(TOKENS, QHEADS * DH)
    key_grad = key_total[front:] * inv_root
    value_grad = value_total[front:]
    return (output, query_grad, key_grad, value_grad)
```

```python
import math

import jax
import jax.numpy as jnp
from jax import lax
from jax.experimental import pallas as pl
from jax.experimental.pallas import tpu as pltpu
from jax.sharding import PartitionSpec as P

DOC_CAP = 4096
NEG = -1e30
CHUNK = 128

VMEM = pl.BlockSpec(memory_space=pltpu.VMEM)
SMEM = pl.BlockSpec(memory_space=pltpu.SMEM)


def nt(a, b):
    return lax.dot_general(a, b, (((1,), (1,)), ((), ())), preferred_element_type=jnp.float32)


def nn(a, b):
    return lax.dot_general(a, b, (((1,), (0,)), ((), ())), preferred_element_type=jnp.float32)


def tn(a, b):
    return lax.dot_general(a, b, (((0,), (0,)), ((), ())), preferred_element_type=jnp.float32)


def fold(a, op):
    rows = a.shape[0] // 8
    parts = a.reshape(rows, 8, a.shape[1])
    return op(parts, axis=0)


def swap_near(n):
    return [(i, i ^ 1) for i in range(n)]


def swap_near_odd(n):
    pairs = [(0, 0), (n - 1, n - 1)]
    for i in range(1, n - 1, 2):
        pairs += [(i, i + 1), (i + 1, i)]
    return pairs


def swap_far(n):
    return [(i, i ^ 2) for i in range(n)]


def swap_far_odd(n):
    pairs = [(0, 1), (1, 0), (n - 2, n - 1), (n - 1, n - 2)]
    for i in range(2, n - 2, 4):
        pairs += [(i, i + 2), (i + 2, i), (i + 1, i + 3), (i + 3, i + 1)]
    return pairs


def attend_kernel(rounds, tok, heads, head_dim):
    inv_root = 1.0 / math.sqrt(head_dim)
    per_block = tok // CHUNK
    width = heads * head_dim

    def kernel(lens, q_ref, g_ref, k_ref, v_ref, mine_ref, other_ref,
               od_ref, own_out, mine_out, other_out, w_ref):
        here = lax.axis_index("ctx")
        side = lax.axis_index("head")
        first = here * tok
        places = first + lax.broadcasted_iota(jnp.int32, (1, tok), 1)
        begin = jnp.zeros((1, tok), jnp.int32)
        bound = jnp.int32(0)
        for i in range(lens.shape[0]):
            bound = bound + lens[i]
            begin = jnp.where(places >= bound, bound, begin)

        def own_chunk(c):
            rows = pl.ds(c * CHUNK, CHUNK)
            return k_ref[rows, :], v_ref[rows, :]

        def far_chunk(ref, r, c):
            rows = pl.ds(c * CHUNK, CHUNK)
            return ref[r, rows, :head_dim], ref[r, rows, head_dim:]

        def each(body, carry):
            for c in range(per_block):
                carry = body(own_chunk(c), first + c * CHUNK, c,
                             (own_out, None, c), carry)
            for which, (ref, out) in enumerate(((mine_ref, mine_out), (other_ref, other_out))):
                def one(r, carry):
                    hop = 2 * r + 1 + (side if which == 0 else 1 - side)
                    base = first - hop * tok
                    for c in range(per_block):
                        slot = per_block * (1 + which * rounds + r) + c
                        carry = body(far_chunk(ref, r, c), base + c * CHUNK, slot,
                                     (out, r, c), carry)
                    return carry
                carry = one(0, carry) if rounds == 1 else lax.fori_loop(0, rounds, one, carry)
            return carry

        q = [q_ref[:, h * head_dim:(h + 1) * head_dim] for h in range(heads)]
        g = [g_ref[:, h * head_dim:(h + 1) * head_dim] for h in range(heads)]

        def scores(kv, base, slot, out, tops):
            at = base + lax.broadcasted_iota(jnp.int32, (CHUNK, tok), 0)
            allowed = (at >= begin) & (at <= places)
            result = []
            for h in range(heads):
                s = jnp.where(allowed, nt(kv[0], q[h]) * inv_root, NEG)
                w_ref[h, slot] = s
                result.append(jnp.maximum(tops[h], fold(s, jnp.max)))
            return tuple(result)

        tops = each(scores, tuple(jnp.full((8, tok), NEG, jnp.float32) for _ in range(heads)))
        tops = [jnp.max(t, axis=0, keepdims=True) for t in tops]

        def exps(kv, base, slot, out, totals):
            result = []
            for h in range(heads):
                e = jnp.exp(w_ref[h, slot] - tops[h])
                w_ref[h, slot] = e
                result.append(totals[h] + fold(e, jnp.sum))
            return tuple(result)

        totals = each(exps, tuple(jnp.zeros((8, tok), jnp.float32) for _ in range(heads)))
        scale = [1.0 / jnp.sum(t, axis=0, keepdims=True) for t in totals]

        def values(kv, base, slot, out, acc):
            result = []
            for h in range(heads):
                w = w_ref[h, slot] * scale[h]
                w_ref[h, slot] = w
                result.append(acc[h] + tn(kv[1], w.astype(jnp.bfloat16)))
            return tuple(result)

        acc = each(values, tuple(jnp.zeros((head_dim, tok), jnp.float32) for _ in range(heads)))
        dots = []
        for h in range(heads):
            attended = acc[h].T.astype(jnp.bfloat16)
            od_ref[:, h * head_dim:(h + 1) * head_dim] = attended
            product = g[h].astype(jnp.float32) * attended.astype(jnp.float32)
            dots.append(jnp.sum(product.T, axis=0, keepdims=True))

        def backward(kv, base, slot, out, acc):
            result = []
            key_term = value_term = None
            for h in range(heads):
                w = w_ref[h, slot]
                ds = (w * (nt(kv[1], g[h]) - dots[h])).astype(jnp.bfloat16)
                result.append(acc[h] + tn(kv[0], ds))
                dk = nn(ds, q[h])
                dv = nn(w.astype(jnp.bfloat16), g[h])
                key_term = dk if h == 0 else key_term + dk
                value_term = dv if h == 0 else value_term + dv
            ref, r, c = out
            rows = pl.ds(c * CHUNK, CHUNK)
            key_term = (key_term * inv_root).astype(ref.dtype)
            value_term = value_term.astype(ref.dtype)
            if r is None:
                ref[rows, :head_dim] = key_term
                ref[rows, head_dim:] = value_term
            else:
                ref[r, rows, :head_dim] = key_term
                ref[r, rows, head_dim:] = value_term
            return tuple(result)

        acc = each(backward, tuple(jnp.zeros((head_dim, tok), jnp.float32) for _ in range(heads)))
        for h in range(heads):
            od_ref[:, width + h * head_dim:width + (h + 1) * head_dim] = (
                (acc[h] * inv_root).T.astype(jnp.bfloat16))

    return kernel


def place_kernel(n, stretch, width):
    def kernel(plan, own, near, near_odd, far, far_odd, x_ref, y_ref,
               out_ref, dq_ref, dk_ref, dv_ref):
        here = lax.axis_index("ctx")
        odd = here % 2
        upper = (here // 2) % 2
        near_odd_src = jnp.clip(here + 2 * odd - 1, 0, n - 1)
        inner = (here >= 2) & (here < n - 2)
        far_odd_src = jnp.where(inner, here + 4 * upper - 2, here + 1 - 2 * odd)
        sources = ((own, here), (near, here + 1 - 2 * odd), (near_odd, near_odd_src),
                   (far, here + 2 - 4 * upper), (far_odd, far_odd_src))
        for slot in range(2):
            wanted = plan[slot]
            rows = pl.ds(pl.multiple_of((wanted % 2) * stretch, stretch), stretch)
            to = pl.ds(slot * stretch, stretch)
            for ref, source in sources:
                @pl.when(wanted // 2 == source)
                def _():
                    out_ref[to, :] = ref[rows, :width]
                    dq_ref[to, :] = ref[rows, width:].astype(jnp.float32)
        half = dk_ref.shape[1]
        dk_ref[...] = x_ref[:, :half] + y_ref[:, :half]
        dv_ref[...] = x_ref[:, half:] + y_ref[:, half:]

    return kernel


def per_device(queries, key_input, value_input, grad_out, doc_lengths, stretch_plan):
    tok, head_dim = key_input.shape
    width = queries.shape[1]
    heads = width // head_dim
    n = lax.axis_size("ctx")
    reach = min(DOC_CAP, tok * n // 4) // tok
    rounds = (reach + 1) // 2
    bf16, f32 = jnp.bfloat16, jnp.float32
    both = ("ctx", "head")
    cross = [(0, 1), (1, 0)]

    def hop_pairs(r, back):
        pairs = []
        for s in range(n):
            for h in range(2):
                to = s + 2 * r + 1 + h
                if to < n:
                    a, b = 2 * s + h, 2 * to + h
                    pairs.append((b, a) if back else (a, b))
        return pairs

    own_kv = jnp.concatenate([key_input, value_input], axis=1)
    mine = jnp.stack([lax.ppermute(own_kv, both, hop_pairs(r, False)) for r in range(rounds)])
    other = lax.ppermute(mine, "head", cross)

    blocks = 1 + 2 * rounds
    od, own_part, mine_part, other_part = pl.pallas_call(
        attend_kernel(rounds, tok, heads, head_dim),
        out_shape=(
            jax.ShapeDtypeStruct((tok, 2 * width), bf16),
            jax.ShapeDtypeStruct((tok, 2 * head_dim), f32),
            jax.ShapeDtypeStruct((rounds, tok, 2 * head_dim), bf16),
            jax.ShapeDtypeStruct((rounds, tok, 2 * head_dim), bf16),
        ),
        in_specs=[SMEM] + [VMEM] * 6,
        out_specs=(VMEM,) * 4,
        scratch_shapes=[pltpu.VMEM((heads, blocks * (tok // CHUNK), CHUNK, tok), f32)],
        compiler_params=pltpu.CompilerParams(vmem_limit_bytes=40 << 20),
        name="attend",
    )(doc_lengths, queries, grad_out, key_input, value_input, mine, other)

    partner = lax.ppermute(other_part, "head", cross)
    back = (mine_part.astype(f32) + partner.astype(f32)).astype(bf16)
    total = own_part
    for r in range(rounds):
        total = total + lax.ppermute(back[r], both, hop_pairs(r, True)).astype(f32)
    moved = [lax.ppermute(od, "ctx", pairs(n))
             for pairs in (swap_near, swap_near_odd, swap_far, swap_far_odd)]
    total_other = lax.ppermute(total, "head", cross)

    output, query_grad, key_grad, value_grad = pl.pallas_call(
        place_kernel(n, tok // 2, width),
        out_shape=(
            jax.ShapeDtypeStruct((tok, width), bf16),
            jax.ShapeDtypeStruct((tok, width), f32),
            jax.ShapeDtypeStruct((tok, head_dim), f32),
            jax.ShapeDtypeStruct((tok, head_dim), f32),
        ),
        in_specs=[SMEM] + [VMEM] * 7,
        out_specs=(VMEM,) * 4,
        name="place",
    )(stretch_plan, od, *moved, total, total_other)
    return (output, query_grad, key_grad, value_grad)


def solution(mesh):
    return jax.shard_map(
        per_device,
        mesh=mesh,
        in_specs=(
            P(("groups", "ctx"), "head"),
            P(("groups", "ctx"), None),
            P(("groups", "ctx"), None),
            P(("groups", "ctx"), "head"),
            P("groups"),
            P(("groups", "ctx")),
        ),
        out_specs=(
            P(("groups", "ctx"), "head"),
            P(("groups", "ctx"), "head"),
            P(("groups", "ctx"), None),
            P(("groups", "ctx"), None),
        ),
        check_vma=False,
    )
```

```python
import math

import jax
import jax.numpy as jnp
from jax import lax
from jax.experimental import pallas as pl
from jax.experimental.pallas import tpu as pltpu
from jax.sharding import PartitionSpec as P

DOC_CAP = 4096
NEG = -1e30
LOG2E = 1.4426950408889634
CHUNK = 128

VMEM = pl.BlockSpec(memory_space=pltpu.VMEM)
SMEM = pl.BlockSpec(memory_space=pltpu.SMEM)


def nt(a, b):
    return lax.dot_general(a, b, (((1,), (1,)), ((), ())), preferred_element_type=jnp.float32)


def nn(a, b):
    return lax.dot_general(a, b, (((1,), (0,)), ((), ())), preferred_element_type=jnp.float32)


def tn(a, b):
    return lax.dot_general(a, b, (((0,), (0,)), ((), ())), preferred_element_type=jnp.float32)


def fold(a, op):
    rows = a.shape[0] // 8
    parts = a.reshape(rows, 8, a.shape[1])
    return op(parts, axis=0)


def up_down(z, flip):
    return z + 1 - 2 * ((z + flip) % 2)


def row_pairs(rows):
    pairs = ([], [])
    for z in range(rows):
        for x in range(2):
            for h in range(2):
                for way in range(2):
                    to = z + 1 - 2 * ((z + (h ^ way)) % 2)
                    other = (to, x) if 0 <= to < rows else (z, 1 - x)
                    node = 4 * z + 2 * x + h
                    pairs[way].append((node, 4 * other[0] + 2 * other[1] + h))
    return pairs


def pack_kernel(k_ref, v_ref, q_ref, g_ref, kv_ref, bundle_ref, sems):
    side = lax.axis_index("head")
    dim = k_ref.shape[1]
    width = q_ref.shape[1]
    half = bundle_ref.at[:, 2 * width:]
    moves = (
        (k_ref, kv_ref.at[:, :dim]),
        (v_ref, kv_ref.at[:, dim:]),
        (q_ref, bundle_ref.at[:, :width]),
        (g_ref, bundle_ref.at[:, width:2 * width]),
    )
    copies = [pltpu.make_async_copy(a, b, sems.at[i]) for i, (a, b) in enumerate(moves)]
    for copy in copies:
        copy.start()
    for copy in copies[:2]:
        copy.wait()

    @pl.when(side == 0)
    def _():
        half[...] = kv_ref[:, :dim]

    @pl.when(side == 1)
    def _():
        half[...] = kv_ref[:, dim:]

    for copy in copies[2:]:
        copy.wait()


def loop(count, body, carry):
    if count <= 8:
        for j in range(count):
            carry = body(j, carry)
        return carry
    return lax.fori_loop(0, count, body, carry)

def rows_at(c):
    start = c * CHUNK
    return pl.ds(start if isinstance(start, int) else pl.multiple_of(start, CHUNK), CHUNK)


def two_stretches(sizes, lens, z, column, kbuf, vbuf, q_all, g_all, w_ref, p_ref, d_ref,
                  od_ref, put=None):
    rounds, reach, tok, heads, head_dim = sizes
    inv_root = 1.0 / math.sqrt(head_dim)
    width = heads * head_dim
    lanes = heads * CHUNK
    span = 2 * reach + 2
    unrolled = span <= 8
    low = 4 * rounds + 2 * column - 2 * reach
    low_place = (2 * (z - rounds) * tok) + low * CHUNK
    q, g, places, begin = [], [], [], []
    for i in range(2):
        rows = slice(i * CHUNK, (i + 1) * CHUNK)
        q.append(jnp.concatenate(
            [q_all[rows, h * head_dim:(h + 1) * head_dim] for h in range(heads)], axis=0))
        g.append(jnp.concatenate(
            [g_all[rows, h * head_dim:(h + 1) * head_dim] for h in range(heads)], axis=0))
        lane = lax.broadcasted_iota(jnp.int32, (1, lanes), 1) % CHUNK
        place = (2 * z + column) * tok + i * CHUNK + lane
        start = jnp.zeros((1, lanes), jnp.int32)
        bound = jnp.int32(0)
        for m in range(lens.shape[0]):
            bound = bound + lens[m]
            start = jnp.where(place >= bound, bound, start)
        places.append(place)
        begin.append(start)

    def slots(j):
        if not unrolled:
            return (0, 1)
        return tuple(i for i in range(2) if i <= j <= 2 * reach + i)

    def of_slot(i):
        return slice(i * lanes, (i + 1) * lanes)

    def contract(buf, ref, i):
        if unrolled:
            rows = (2 * reach + 1) * CHUNK
            at = pl.ds(pl.multiple_of((low + i) * CHUNK, CHUNK), rows)
            return tn(buf[at, :], ref[i * CHUNK:i * CHUNK + rows, of_slot(i)])

        def add(j, acc):
            return acc + tn(buf[rows_at(low + j), :], ref[rows_at(j), of_slot(i)])

        return lax.fori_loop(0, span, add, jnp.zeros((head_dim, lanes), jnp.float32))

    def scores(j, tops):
        tops = list(tops)
        k = kbuf[rows_at(low + j), :]
        at = low_place + j * CHUNK + lax.broadcasted_iota(jnp.int32, (CHUNK, lanes), 0)
        for i in slots(j):
            allowed = at >= begin[i]
            if not unrolled or j == 2 * reach + i:
                allowed = allowed & (at <= places[i])
            s = jnp.where(allowed, nt(k, q[i]) * (inv_root * LOG2E), NEG)
            w_ref[i, j] = s
            tops[i] = jnp.maximum(tops[i], fold(s, jnp.max))
        return tuple(tops)

    full = lambda value: tuple(jnp.full((8, lanes), value, jnp.float32) for _ in range(2))
    tops = loop(span, scores, full(NEG))
    tops = [jnp.max(t, axis=0, keepdims=True) for t in tops]

    def exps(j, totals):
        totals = list(totals)
        for i in slots(j):
            e = jnp.exp2(w_ref[i, j] - tops[i])
            w_ref[i, j] = e
            p_ref[rows_at(j), of_slot(i)] = e.astype(jnp.bfloat16)
            totals[i] = totals[i] + fold(e, jnp.sum)
        return tuple(totals)

    totals = loop(span, exps, full(0.0))
    scale = [1.0 / jnp.sum(t, axis=0, keepdims=True) for t in totals]
    dots = []
    for i in range(2):
        attended = (contract(vbuf, p_ref, i) * scale[i]).T.astype(jnp.bfloat16)
        for h in range(heads):
            od_ref[i * CHUNK:(i + 1) * CHUNK, h * head_dim:(h + 1) * head_dim] = (
                attended[h * CHUNK:(h + 1) * CHUNK])
        product = g[i].astype(jnp.float32) * attended.astype(jnp.float32)
        dots.append(jnp.sum(product.T, axis=0, keepdims=True))

    def backward(j, carry):
        v = vbuf[rows_at(low + j), :]
        for i in range(2):
            if i in slots(j):
                w = w_ref[i, j] * scale[i]
                ds = (w * (nt(v, g[i]) - dots[i])).astype(jnp.bfloat16)
                d_ref[rows_at(j), of_slot(i)] = ds
                if put is not None:
                    p_ref[rows_at(j), of_slot(i)] = w.astype(jnp.bfloat16)
            elif put is not None:
                blank = jnp.zeros((CHUNK, lanes), jnp.bfloat16)
                d_ref[rows_at(j), of_slot(i)] = blank
                p_ref[rows_at(j), of_slot(i)] = blank
        return carry

    loop(span, backward, 0)
    if put is not None:
        q_both = jnp.concatenate(q, axis=0)
        g_both = jnp.concatenate(g, axis=0)

        def keys(b, carry):
            start = b * tok
            at = pl.ds(start if isinstance(start, int) else pl.multiple_of(start, tok), tok)
            put(reach - b, nn(d_ref[at, :], q_both) * inv_root, nn(p_ref[at, :], g_both))
            return carry

        loop(reach + 1, keys, 0)
    for i in range(2):
        grad = (contract(kbuf, d_ref, i) * inv_root).T.astype(jnp.bfloat16)
        for h in range(heads):
            at = width + h * head_dim
            od_ref[i * CHUNK:(i + 1) * CHUNK, at:at + head_dim] = (
                grad[h * CHUNK:(h + 1) * CHUNK])


def own_kernel(sizes):
    rounds, reach, tok, heads, head_dim = sizes

    def kernel(lens, k_ref, v_ref, q_ref, g_ref, mine_ref, other_ref, part_ref, cross_ref,
               od_ref, own_out, mine_out, other_out, kbuf, vbuf, w_ref, p_ref, d_ref, grads):
        here = lax.axis_index("ctx")
        side = lax.axis_index("head")
        z = here // 2
        x = here % 2
        half = part_ref.at[:, 2 * heads * head_dim:]

        for r in range(rounds):
            for ref, column in ((mine_ref, (x + side) % 2), (other_ref, (x + 1 - side) % 2)):
                at = pl.ds(pl.multiple_of((2 * (rounds - 1 - r) + column) * tok, tok), tok)
                kbuf[at, :] = ref[r, :, :head_dim]
                vbuf[at, :] = ref[r, :, head_dim:]
        own = pl.ds(pl.multiple_of((2 * rounds + x) * tok, tok), tok)
        kbuf[own, :] = k_ref[...]
        vbuf[own, :] = v_ref[...]
        next_to = pl.ds(pl.multiple_of((2 * rounds + 1 - x) * tok, tok), tok)

        @pl.when(side == 0)
        def _():
            kbuf[next_to, :] = half[...]
            vbuf[next_to, :] = cross_ref[...]

        @pl.when(side == 1)
        def _():
            vbuf[next_to, :] = half[...]
            kbuf[next_to, :] = cross_ref[...]

        def put(hop, dk, dv):
            def own_block():
                own_out[:, :head_dim] = dk
                own_out[:, head_dim:] = dv

            def far_block():
                grads[hop - 1, :, :head_dim] = dk.astype(grads.dtype)
                grads[hop - 1, :, head_dim:] = dv.astype(grads.dtype)

            if isinstance(hop, int):
                own_block() if hop == 0 else far_block()
            else:
                pl.when(hop == 0)(own_block)
                pl.when(hop > 0)(far_block)

        if reach < 2 * rounds:
            grads[reach] = jnp.zeros(grads.shape[1:], grads.dtype)
        two_stretches(sizes, lens, z, x, kbuf, vbuf, q_ref, g_ref, w_ref, p_ref, d_ref, od_ref, put)
        for r in range(rounds):
            mine_out[r] = grads[2 * r + side]
            other_out[r] = grads[2 * r + 1 - side]

    return kernel


def next_kernel(sizes):
    rounds, reach, tok, heads, head_dim = sizes
    width = heads * head_dim

    def kernel(lens, plan, kbuf, vbuf, qg_ref, own_od, od_ref, send_a, send_b, w_ref, p_ref, d_ref):
        here = lax.axis_index("ctx")
        side = lax.axis_index("head")
        z = here // 2
        x = here % 2
        od_ref[:tok, :] = own_od[...]
        two_stretches(sizes, lens, z, 1 - x, kbuf, vbuf, qg_ref.at[:, :width],
                      qg_ref.at[:, width:2 * width], w_ref, p_ref, d_ref, od_ref.at[tok:, :])
        for way, out in enumerate((send_a, send_b)):
            flip = (side + way) % 2
            for i in range(2):
                wanted = jnp.where(flip == 0, plan[i], plan[2 + i])
                at = row_of(wanted, x)
                out[i * CHUNK:(i + 1) * CHUNK, :] = od_ref[at, :]

    return kernel


def row_of(wanted, x):
    inner = wanted % 4
    return pl.ds(pl.multiple_of(((inner + 2 * x) % 4) * CHUNK, CHUNK), CHUNK)


def place_kernel(width):
    def kernel(plan, row_ref, a_ref, b_ref, s_ref, t_ref, out_ref, dq_ref, dk_ref, dv_ref):
        here = lax.axis_index("ctx")
        side = lax.axis_index("head")
        z = here // 2
        source_a = up_down(z, side)
        for slot in range(2):
            wanted = plan[slot]
            to = pl.ds(slot * CHUNK, CHUNK)
            inside = row_of(wanted, here % 2)

            def put(rows):
                out_ref[to, :] = rows[:, :width]
                dq_ref[to, :] = rows[:, width:].astype(jnp.float32)

            home = wanted // 4 == z
            from_a = wanted // 4 == source_a
            pl.when(home)(lambda: put(row_ref[inside, :]))
            pl.when(from_a)(lambda: put(a_ref[to, :]))
            pl.when(jnp.logical_not(home | from_a))(lambda: put(b_ref[to, :]))
        half = dk_ref.shape[1]
        dk_ref[...] = s_ref[:, :half] + t_ref[:, :half]
        dv_ref[...] = s_ref[:, half:] + t_ref[:, half:]

    return kernel


def per_device(queries, key_input, value_input, grad_out, doc_lengths, stretch_plan):
    tok, head_dim = key_input.shape
    width = queries.shape[1]
    heads = width // head_dim
    n = lax.axis_size("ctx")
    reach = min(DOC_CAP, tok * n // 4) // tok
    rounds = (reach + 1) // 2
    bf16, f32 = jnp.bfloat16, jnp.float32
    both = ("ctx", "head")
    cross = [(0, 1), (1, 0)]
    side = lax.axis_index("head")

    def fetch_pairs(r):
        pairs = []
        for s in range(n):
            for h in range(2):
                to = s // 2 + r + 1
                if to < n // 2:
                    pairs.append((2 * s + h, 2 * (2 * to + (s + h) % 2) + h))
        return pairs

    def back_pairs(r):
        pairs = []
        for s in range(n):
            for h in range(2):
                to = s - (2 * r + 1 + h)
                if to >= 0:
                    pairs.append((2 * s + h, 2 * to + h))
        return pairs

    own_kv, bundle = pl.pallas_call(
        pack_kernel,
        out_shape=(
            pltpu.VMEM((tok, 2 * head_dim), bf16),
            pltpu.VMEM((tok, 2 * width + head_dim), bf16),
        ),
        in_specs=[pl.BlockSpec(memory_space=pl.ANY)] * 4,
        out_specs=(VMEM,) * 2,
        scratch_shapes=[pltpu.SemaphoreType.DMA((4,))],
        name="pack",
    )(key_input, value_input, queries, grad_out)
    tie_a, tie_b = row_pairs(n // 2)
    part = lax.ppermute(bundle, "ctx", [(i, i ^ 1) for i in range(n)])
    mine = [lax.ppermute(own_kv, both, fetch_pairs(r)) for r in range(rounds)]
    plan_mine = lax.ppermute(stretch_plan, both, tie_a)
    *mine, part, plan_mine = lax.optimization_barrier((*mine, part, plan_mine))
    mine = jnp.stack(mine)
    other = lax.ppermute(mine, "head", cross)
    half_cross = lax.ppermute(part[:, 2 * width:], "head", cross)
    plan_other = lax.ppermute(plan_mine, "head", cross)
    plans = jnp.where(side == 0, jnp.concatenate([plan_mine, plan_other]),
                      jnp.concatenate([plan_other, plan_mine]))

    other, half_cross, plans = lax.optimization_barrier((other, half_cross, plans))
    sizes = (rounds, reach, tok, heads, head_dim)
    params = pltpu.CompilerParams(vmem_limit_bytes=40 << 20)
    span = 2 * reach + 2
    weights = pltpu.VMEM((span * CHUNK, 2 * heads * CHUNK), bf16)
    scores = [pltpu.VMEM((2, span, CHUNK, heads * CHUNK), f32), weights, weights]
    buffer = jax.ShapeDtypeStruct(((2 * rounds + 2) * tok, head_dim), bf16)
    rows = jax.ShapeDtypeStruct((tok, 2 * width), bf16)
    far = jax.ShapeDtypeStruct((rounds, tok, 2 * head_dim), bf16)
    od_own, own_part, mine_part, other_part, kbuf, vbuf = pl.pallas_call(
        own_kernel(sizes),
        out_shape=(rows, jax.ShapeDtypeStruct((tok, 2 * head_dim), f32), far, far, buffer, buffer),
        in_specs=[SMEM] + [VMEM] * 8,
        out_specs=(VMEM,) * 6,
        scratch_shapes=scores + [pltpu.VMEM((2 * rounds, tok, 2 * head_dim), bf16)],
        compiler_params=params,
        name="attend_own",
    )(doc_lengths, key_input, value_input, queries, grad_out, mine, other, part, half_cross)
    partner = lax.ppermute(other_part, "head", cross)
    od, send_a, send_b = pl.pallas_call(
        next_kernel(sizes),
        out_shape=(jax.ShapeDtypeStruct((2 * tok, 2 * width), bf16), rows, rows),
        in_specs=[SMEM, SMEM] + [VMEM] * 4,
        out_specs=(VMEM,) * 3,
        scratch_shapes=scores,
        compiler_params=params,
        name="attend_next",
    )(doc_lengths, plans, kbuf, vbuf, part, od_own)

    moved_a = lax.ppermute(send_a, both, tie_a)
    moved_b = lax.ppermute(send_b, both, tie_b)
    back = (mine_part.astype(f32) + partner.astype(f32)).astype(bf16)
    total = own_part
    for r in range(rounds):
        total = total + lax.ppermute(back[r], both, back_pairs(r)).astype(f32)
    total_other = lax.ppermute(total, "head", cross)

    output, query_grad, key_grad, value_grad = pl.pallas_call(
        place_kernel(width),
        out_shape=(
            jax.ShapeDtypeStruct((tok, width), bf16),
            jax.ShapeDtypeStruct((tok, width), f32),
            jax.ShapeDtypeStruct((tok, head_dim), f32),
            jax.ShapeDtypeStruct((tok, head_dim), f32),
        ),
        in_specs=[SMEM] + [VMEM] * 5,
        out_specs=(VMEM,) * 4,
        compiler_params=pltpu.CompilerParams(vmem_limit_bytes=32 << 20),
        name="place",
    )(stretch_plan, od, moved_a, moved_b, total, total_other)
    return (output, query_grad, key_grad, value_grad)


def solution(mesh):
    return jax.shard_map(
        per_device,
        mesh=mesh,
        in_specs=(
            P(("groups", "ctx"), "head"),
            P(("groups", "ctx"), None),
            P(("groups", "ctx"), None),
            P(("groups", "ctx"), "head"),
            P("groups"),
            P(("groups", "ctx")),
        ),
        out_specs=(
            P(("groups", "ctx"), "head"),
            P(("groups", "ctx"), "head"),
            P(("groups", "ctx"), None),
            P(("groups", "ctx"), None),
        ),
        check_vma=False,
    )
```

```python
import math

import jax
import jax.numpy as jnp
from jax import lax
from jax.experimental import pallas as pl
from jax.experimental.pallas import tpu as pltpu
from jax.sharding import PartitionSpec as P

DOC_CAP = 4096
NEG = -1e30


LOG2E = 1.4426950408889634
CHUNK = 128

VMEM = pl.BlockSpec(memory_space=pltpu.VMEM)
SMEM = pl.BlockSpec(memory_space=pltpu.SMEM)


def nt(a, b):
    return lax.dot_general(a, b, (((1,), (1,)), ((), ())), preferred_element_type=jnp.float32)


def nn(a, b):
    return lax.dot_general(a, b, (((1,), (0,)), ((), ())), preferred_element_type=jnp.float32)


def tn(a, b):
    return lax.dot_general(a, b, (((0,), (0,)), ((), ())), preferred_element_type=jnp.float32)


def fold(a, op):
    rows = a.shape[0] // 8
    parts = a.reshape(rows, 8, a.shape[1])
    return op(parts, axis=0)


def scalars(ref, count):
    row = ref[...]
    lane = lax.broadcasted_iota(jnp.int32, row.shape, 1)
    return [jnp.sum(jnp.where(lane == i, row, 0)) for i in range(count)]


def up_down(z, flip):
    return z + 1 - 2 * ((z + flip) % 2)


def row_pairs(rows):
    pairs = ([], [])
    for z in range(rows):
        for x in range(2):
            for h in range(2):
                for way in range(2):
                    to = z + 1 - 2 * ((z + (h ^ way)) % 2)
                    other = (to, x) if 0 <= to < rows else (z, 1 - x)
                    node = 4 * z + 2 * x + h
                    pairs[way].append((node, 4 * other[0] + 2 * other[1] + h))
    return pairs


def pack_kernel(plan_ref, k_ref, v_ref, q_ref, g_ref, plan_out, kv_ref, half_ref, qg_ref, sems):
    side = lax.axis_index("head")
    dim = k_ref.shape[1]
    width = q_ref.shape[1]
    moves = (
        (k_ref, kv_ref.at[:, :dim]),
        (v_ref, kv_ref.at[:, dim:]),
        (q_ref, qg_ref.at[:, :width]),
        (g_ref, qg_ref.at[:, width:]),
        (plan_ref, plan_out),
    )
    copies = [pltpu.make_async_copy(a, b, sems.at[i]) for i, (a, b) in enumerate(moves)]
    for copy in copies:
        copy.start()
    for copy in copies[:2]:
        copy.wait()

    @pl.when(side == 0)
    def _():
        half_ref[...] = kv_ref[:, :dim]

    @pl.when(side == 1)
    def _():
        half_ref[...] = kv_ref[:, dim:]

    for copy in copies[2:]:
        copy.wait()


def loop(count, body, carry):
    if count <= 8:
        for j in range(count):
            carry = body(j, carry)
        return carry
    return lax.fori_loop(0, count, body, carry)

def rows_at(c):
    start = c * CHUNK
    return pl.ds(start if isinstance(start, int) else pl.multiple_of(start, CHUNK), CHUNK)


def contract(sizes, low, buf, ref, i):
    rounds, reach, tok, heads, head_dim = sizes
    lanes = heads * CHUNK
    span = 2 * reach + 2
    slot = slice(i * lanes, (i + 1) * lanes)
    if span <= 8:
        rows = (2 * reach + 1) * CHUNK
        at = pl.ds(pl.multiple_of((low + i) * CHUNK, CHUNK), rows)
        return tn(buf[at, :], ref[i * CHUNK:i * CHUNK + rows, slot])

    def add(j, acc):
        return acc + tn(buf[rows_at(low + j), :], ref[rows_at(j), slot])

    return lax.fori_loop(0, span, add, jnp.zeros((head_dim, lanes), jnp.float32))


def two_stretches(sizes, begin_ref, z, column, kbuf, vbuf, q_all, g_all, w_ref, p_ref, d_ref,
                  od_ref, blocks, put):
    rounds, reach, tok, heads, head_dim = sizes
    inv_root = 1.0 / math.sqrt(head_dim)
    width = heads * head_dim
    lanes = heads * CHUNK
    span = 2 * reach + 2
    unrolled = span <= 8
    low = 4 * rounds + 2 * column - 2 * reach
    low_place = (2 * (z - rounds) * tok) + low * CHUNK
    q, g, places, begin = [], [], [], []
    for i in range(2):
        rows = slice(i * CHUNK, (i + 1) * CHUNK)
        q.append(jnp.concatenate(
            [q_all[rows, h * head_dim:(h + 1) * head_dim] for h in range(heads)], axis=0))
        g.append(jnp.concatenate(
            [g_all[rows, h * head_dim:(h + 1) * head_dim] for h in range(heads)], axis=0))
        lane = lax.broadcasted_iota(jnp.int32, (1, lanes), 1) % CHUNK
        place = (2 * z + column) * tok + i * CHUNK + lane
        places.append(place)
        begin.append(begin_ref[i:i + 1, :])

    def slots(j):
        if not unrolled:
            return (0, 1)
        return tuple(i for i in range(2) if i <= j <= 2 * reach + i)

    def scores(j, tops):
        tops = list(tops)
        k = kbuf[rows_at(low + j), :]
        at = low_place + j * CHUNK + lax.broadcasted_iota(jnp.int32, (CHUNK, lanes), 0)
        for i in slots(j):
            allowed = at >= begin[i]
            if not unrolled or j == 2 * reach + i:
                allowed = allowed & (at <= places[i])
            s = jnp.where(allowed, nt(k, q[i]) * (inv_root * LOG2E), NEG)
            w_ref[i, j] = s
            tops[i] = jnp.maximum(tops[i], fold(s, jnp.max))
        return tuple(tops)

    full = lambda value: tuple(jnp.full((8, lanes), value, jnp.float32) for _ in range(2))
    tops = loop(span, scores, full(NEG))
    tops = [jnp.max(t, axis=0, keepdims=True) for t in tops]

    def exps(j, totals):
        totals = list(totals)
        for i in slots(j):
            e = jnp.exp2(w_ref[i, j] - tops[i])
            w_ref[i, j] = e
            p_ref[rows_at(j), slice(i * lanes, (i + 1) * lanes)] = e.astype(jnp.bfloat16)
            totals[i] = totals[i] + fold(e, jnp.sum)
        return tuple(totals)

    totals = loop(span, exps, full(0.0))
    scale = [1.0 / jnp.sum(t, axis=0, keepdims=True) for t in totals]
    dots = []
    for i in range(2):
        attended = (contract(sizes, low, vbuf, p_ref, i) * scale[i]).T.astype(jnp.bfloat16)
        for h in range(heads):
            od_ref[i * CHUNK:(i + 1) * CHUNK, h * head_dim:(h + 1) * head_dim] = (
                attended[h * CHUNK:(h + 1) * CHUNK])
        product = g[i].astype(jnp.float32) * attended.astype(jnp.float32)
        dots.append(jnp.sum(product.T, axis=0, keepdims=True))

    def backward(j, carry):
        v = vbuf[rows_at(low + j), :]
        for i in range(2):
            if i in slots(j):
                w = w_ref[i, j] * scale[i]
                ds = (w * (nt(v, g[i]) - dots[i])).astype(jnp.bfloat16)
                d_ref[rows_at(j), slice(i * lanes, (i + 1) * lanes)] = ds
                p_ref[rows_at(j), slice(i * lanes, (i + 1) * lanes)] = w.astype(jnp.bfloat16)
            else:
                blank = jnp.zeros((CHUNK, lanes), jnp.bfloat16)
                d_ref[rows_at(j), slice(i * lanes, (i + 1) * lanes)] = blank
                p_ref[rows_at(j), slice(i * lanes, (i + 1) * lanes)] = blank
        return carry

    loop(span, backward, 0)
    q_both = jnp.concatenate(q, axis=0)
    g_both = jnp.concatenate(g, axis=0)

    def keys(m, carry):
        first, count = blocks
        b = first + 2 * m
        start = b * tok
        at = pl.ds(start if isinstance(start, int) else pl.multiple_of(start, tok), tok)
        put(count - 1 - m, nn(d_ref[at, :], q_both) * inv_root, nn(p_ref[at, :], g_both))
        return carry

    loop(blocks[1], keys, 0)


def query_grads(sizes, column, kbuf, d_ref, od_ref):
    rounds, reach, tok, heads, head_dim = sizes
    inv_root = 1.0 / math.sqrt(head_dim)
    low = 4 * rounds + 2 * column - 2 * reach
    width = heads * head_dim
    for i in range(2):
        grad = (contract(sizes, low, kbuf, d_ref, i) * inv_root).T.astype(jnp.bfloat16)
        for h in range(heads):
            at = width + h * head_dim
            od_ref[i * CHUNK:(i + 1) * CHUNK, at:at + head_dim] = (
                grad[h * CHUNK:(h + 1) * CHUNK])


def own_kernel(sizes):
    rounds, reach, tok, heads, head_dim = sizes

    def kernel(begin_ref, k_ref, v_ref, q_ref, g_ref, mine_ref, other_ref, half_ref, cross_ref,
               att_ref, d_ref, kv_out, kbuf, vbuf, w_ref, p_ref):
        here = lax.axis_index("ctx")
        side = lax.axis_index("head")
        z = here // 2
        x = here % 2

        for r in range(rounds):
            for ref, column in ((mine_ref, (x + side) % 2), (other_ref, (x + 1 - side) % 2)):
                at = pl.ds(pl.multiple_of((2 * (rounds - 1 - r) + column) * tok, tok), tok)
                kbuf[at, :] = ref[r, :, :head_dim]
                vbuf[at, :] = ref[r, :, head_dim:]
        own = pl.ds(pl.multiple_of((2 * rounds + x) * tok, tok), tok)
        kbuf[own, :] = k_ref[...]
        vbuf[own, :] = v_ref[...]
        next_to = pl.ds(pl.multiple_of((2 * rounds + 1 - x) * tok, tok), tok)

        @pl.when(side == 0)
        def _():
            kbuf[next_to, :] = half_ref[...]
            vbuf[next_to, :] = cross_ref[...]

        @pl.when(side == 1)
        def _():
            vbuf[next_to, :] = half_ref[...]
            kbuf[next_to, :] = cross_ref[...]

        def put(r, dk, dv):
            kv_out[r, :, :head_dim] = dk
            kv_out[r, :, head_dim:] = dv

        two_stretches(sizes, begin_ref, z, x, kbuf, vbuf, q_ref, g_ref, w_ref, p_ref, d_ref,
                      att_ref, (0, rounds + 1), put)

    return kernel


def next_kernel(sizes):
    rounds, reach, tok, heads, head_dim = sizes
    width = heads * head_dim

    def kernel(begin_ref, kbuf, vbuf, qg_ref, own_kv, att_ref, d_ref, kv_out, far_out,
               w_ref, p_ref, sums):
        here = lax.axis_index("ctx")
        z = here // 2
        x = here % 2
        sums[...] = own_kv[...]

        def put(r, dk, dv):
            at = r + x
            sums[at, :, :head_dim] = sums[at, :, :head_dim] + dk
            sums[at, :, head_dim:] = sums[at, :, head_dim:] + dv

        two_stretches(sizes, begin_ref, z, 1 - x, kbuf, vbuf, qg_ref.at[:, :width],
                      qg_ref.at[:, width:], w_ref, p_ref, d_ref, att_ref, (1, rounds), put)
        kv_out[...] = sums[0]
        far_out[...] = sums[1:].astype(far_out.dtype)

    return kernel


def send_kernel(sizes):
    rounds, reach, tok, heads, head_dim = sizes
    width = heads * head_dim

    def kernel(plan_ref, kbuf, d_own, d_next, att_own, att_next, od_ref, send_a, send_b):
        here = lax.axis_index("ctx")
        side = lax.axis_index("head")
        x = here % 2
        plan = scalars(plan_ref, 4)
        for at, column, att, d_ref in ((0, x, att_own, d_own), (tok, 1 - x, att_next, d_next)):
            rows = od_ref.at[at:at + tok, :]
            rows[:, :width] = att[...]
            query_grads(sizes, column, kbuf, d_ref, rows)
        for way, out in enumerate((send_a, send_b)):
            flip = (side + way) % 2
            for i in range(2):
                wanted = jnp.where(flip == 0, plan[i], plan[2 + i])
                out[i * CHUNK:(i + 1) * CHUNK, :] = od_ref[row_of(wanted, x), :]

    return kernel


def row_of(wanted, x):
    inner = wanted % 4
    return pl.ds(pl.multiple_of(((inner + 2 * x) % 4) * CHUNK, CHUNK), CHUNK)


def place_kernel(width):
    def kernel(plan_ref, row_ref, a_ref, b_ref, s_ref, t_ref, out_ref, dq_ref, dk_ref, dv_ref):
        here = lax.axis_index("ctx")
        side = lax.axis_index("head")
        z = here // 2
        source_a = up_down(z, side)
        plan = scalars(plan_ref, 2)
        for slot in range(2):
            wanted = plan[slot]
            to = pl.ds(slot * CHUNK, CHUNK)
            inside = row_of(wanted, here % 2)

            def put(rows):
                out_ref[to, :] = rows[:, :width]
                dq_ref[to, :] = rows[:, width:].astype(jnp.float32)

            home = wanted // 4 == z
            from_a = wanted // 4 == source_a
            pl.when(home)(lambda: put(row_ref[inside, :]))
            pl.when(from_a)(lambda: put(a_ref[to, :]))
            pl.when(jnp.logical_not(home | from_a))(lambda: put(b_ref[to, :]))
        half = dk_ref.shape[1]
        dk_ref[...] = s_ref[:, :half] + t_ref[:, :half]
        dv_ref[...] = s_ref[:, half:] + t_ref[:, half:]

    return kernel


def per_device(queries, key_input, value_input, grad_out, doc_lengths, stretch_plan):
    tok, head_dim = key_input.shape
    width = queries.shape[1]
    heads = width // head_dim
    n = lax.axis_size("ctx")
    rounds = (min(DOC_CAP, tok * n // 4) // tok + 1) // 2
    reach = 2 * rounds
    bf16, f32 = jnp.bfloat16, jnp.float32
    both = ("ctx", "head")
    cross = [(0, 1), (1, 0)]
    side = lax.axis_index("head")

    here = lax.axis_index("ctx")
    order = jnp.arange(doc_lengths.shape[0], dtype=jnp.int32)
    bounds = jnp.sum(jnp.where(order[None, :] <= order[:, None], doc_lengths[None, :], 0), axis=1)

    def begins(device):
        places = device * tok + jnp.arange(tok, dtype=jnp.int32)
        starts = jnp.max(jnp.where(bounds[:, None] <= places[None, :], bounds[:, None], 0), axis=0)
        starts = starts.reshape(tok // CHUNK, 1, CHUNK)
        return jnp.broadcast_to(starts, (tok // CHUNK, heads, CHUNK)).reshape(tok // CHUNK, -1)

    def lanes_of(values):
        return jnp.pad(values, (0, 128 - values.shape[0])).reshape(1, 128)

    def fetch_pairs(r):
        pairs = []
        for s in range(n):
            for h in range(2):
                to = s // 2 + r + 1
                if to < n // 2:
                    pairs.append((2 * s + h, 2 * (2 * to + (s + h) % 2) + h))
        return pairs

    def back_pairs(r):
        return [(s, s - 2 * r) for s in range(2 * r, n)]

    plan_out, own_kv, half, queries_grads = pl.pallas_call(
        pack_kernel,
        out_shape=(
            pltpu.VMEM(stretch_plan.shape, jnp.int32),
            pltpu.VMEM((tok, 2 * head_dim), bf16),
            pltpu.VMEM((tok, head_dim), bf16),
            pltpu.VMEM((tok, 2 * width), bf16),
        ),
        in_specs=[pl.BlockSpec(memory_space=pl.ANY)] * 5,
        out_specs=(VMEM,) * 4,
        scratch_shapes=[pltpu.SemaphoreType.DMA((5,))],
        name="pack",
    )(stretch_plan, key_input, value_input, queries, grad_out)
    tie_a, tie_b = row_pairs(n // 2)
    near = [(i, i ^ 1) for i in range(n)]
    part = lax.ppermute(queries_grads, "ctx", near)
    half_next = lax.ppermute(half, "ctx", near)
    mine = [lax.ppermute(own_kv, both, fetch_pairs(r)) for r in range(rounds)]
    mine = jnp.stack(mine)
    other = lax.ppermute(mine, "head", cross)
    half_cross = lax.ppermute(half_next, "head", cross)
    sizes = (rounds, reach, tok, heads, head_dim)
    params = pltpu.CompilerParams(vmem_limit_bytes=40 << 20)
    span = 2 * reach + 2
    weights = pltpu.VMEM((span * CHUNK, 2 * heads * CHUNK), bf16)
    scores = pltpu.VMEM((2, span, CHUNK, heads * CHUNK), f32)
    buffer = jax.ShapeDtypeStruct(((2 * rounds + 2) * tok, head_dim), bf16)
    rows = jax.ShapeDtypeStruct((tok, 2 * width), bf16)
    attended = jax.ShapeDtypeStruct((tok, width), bf16)
    grads = jax.ShapeDtypeStruct((span * CHUNK, 2 * heads * CHUNK), bf16)
    key_sums = jax.ShapeDtypeStruct((rounds + 1, tok, 2 * head_dim), f32)
    att_own, d_own, kv_own, kbuf, vbuf = pl.pallas_call(
        own_kernel(sizes),
        out_shape=(attended, grads, key_sums, buffer, buffer),
        in_specs=[VMEM] * 9,
        out_specs=(VMEM,) * 5,
        scratch_shapes=[scores, weights],
        compiler_params=params,
        name="attend_own",
    )(begins(here), key_input, value_input, queries, grad_out, mine, other, half_next,
      half_cross)
    kv_own, stretch_here = lax.optimization_barrier((kv_own, plan_out))
    plan_mine = lax.ppermute(stretch_here, both, tie_a)
    plan_other = lax.ppermute(plan_mine, "head", cross)
    plans = jnp.where(side == 0, jnp.concatenate([plan_mine, plan_other]),
                      jnp.concatenate([plan_other, plan_mine]))
    att_next, d_next, kv_sum, far = pl.pallas_call(
        next_kernel(sizes),
        out_shape=(
            attended, grads, jax.ShapeDtypeStruct((tok, 2 * head_dim), f32),
            jax.ShapeDtypeStruct((rounds, tok, 2 * head_dim), bf16),
        ),
        in_specs=[VMEM] * 5,
        out_specs=(VMEM,) * 4,
        scratch_shapes=[scores, weights, pltpu.VMEM((rounds + 1, tok, 2 * head_dim), f32)],
        compiler_params=params,
        name="attend_next",
    )(begins(here ^ 1), kbuf, vbuf, part, kv_own)
    od, send_a, send_b = pl.pallas_call(
        send_kernel(sizes),
        out_shape=(jax.ShapeDtypeStruct((2 * tok, 2 * width), bf16), rows, rows),
        in_specs=[VMEM] * 6,
        out_specs=(VMEM,) * 3,
        compiler_params=params,
        name="send_rows",
    )(lanes_of(plans), kbuf, d_own, d_next, att_own, att_next)

    moved_a = lax.ppermute(send_a, both, tie_a)
    moved_b = lax.ppermute(send_b, both, tie_b)
    total = kv_sum
    for r in range(rounds):
        total = total + lax.ppermute(far[r], "ctx", back_pairs(r + 1)).astype(f32)
    total_other = lax.ppermute(total, "head", cross)

    output, query_grad, key_grad, value_grad = pl.pallas_call(
        place_kernel(width),
        out_shape=(
            jax.ShapeDtypeStruct((tok, width), bf16),
            jax.ShapeDtypeStruct((tok, width), f32),
            jax.ShapeDtypeStruct((tok, head_dim), f32),
            jax.ShapeDtypeStruct((tok, head_dim), f32),
        ),
        in_specs=[VMEM] * 6,
        out_specs=(VMEM,) * 4,
        compiler_params=pltpu.CompilerParams(vmem_limit_bytes=32 << 20),
        name="place",
    )(lanes_of(stretch_plan), od, moved_a, moved_b, total, total_other)
    return (output, query_grad, key_grad, value_grad)


def solution(mesh):
    return jax.shard_map(
        per_device,
        mesh=mesh,
        in_specs=(
            P(("groups", "ctx"), "head"),
            P(("groups", "ctx"), None),
            P(("groups", "ctx"), None),
            P(("groups", "ctx"), "head"),
            P("groups"),
            P(("groups", "ctx")),
        ),
        out_specs=(
            P(("groups", "ctx"), "head"),
            P(("groups", "ctx"), "head"),
            P(("groups", "ctx"), None),
            P(("groups", "ctx"), None),
        ),
        check_vma=False,
    )
```

```python
import math

import jax
import jax.numpy as jnp
from jax import lax
from jax.experimental import pallas as pl
from jax.experimental.pallas import tpu as pltpu
from jax.sharding import PartitionSpec as P

DOC_CAP = 4096
NEG = -1e30


LOG2E = 1.4426950408889634
CHUNK = 128

VMEM = pl.BlockSpec(memory_space=pltpu.VMEM)
SMEM = pl.BlockSpec(memory_space=pltpu.SMEM)


def nt(a, b):
    return lax.dot_general(a, b, (((1,), (1,)), ((), ())), preferred_element_type=jnp.float32)


def nn(a, b):
    return lax.dot_general(a, b, (((1,), (0,)), ((), ())), preferred_element_type=jnp.float32)


def tn(a, b):
    return lax.dot_general(a, b, (((0,), (0,)), ((), ())), preferred_element_type=jnp.float32)


def fold(a, op):
    rows = a.shape[0] // 8
    parts = a.reshape(rows, 8, a.shape[1])
    return op(parts, axis=0)


def scalars(ref, count):
    row = ref[...]
    lane = lax.broadcasted_iota(jnp.int32, row.shape, 1)
    return [jnp.sum(jnp.where(lane == i, row, 0)) for i in range(count)]


def up_down(z, flip):
    return z + 1 - 2 * ((z + flip) % 2)


def row_pairs(rows):
    pairs = ([], [])
    for z in range(rows):
        for x in range(2):
            for h in range(2):
                for way in range(2):
                    to = z + 1 - 2 * ((z + (h ^ way)) % 2)
                    other = (to, x) if 0 <= to < rows else (z, 1 - x)
                    node = 4 * z + 2 * x + h
                    pairs[way].append((node, 4 * other[0] + 2 * other[1] + h))
    return pairs


def pack_kernel(plan_ref, k_ref, v_ref, q_ref, g_ref, plan_out, kv_ref, half_ref, qg_ref, sems):
    side = lax.axis_index("head")
    dim = k_ref.shape[1]
    width = q_ref.shape[1]
    moves = (
        (k_ref, kv_ref.at[:, :dim]),
        (v_ref, kv_ref.at[:, dim:]),
        (q_ref, qg_ref.at[:, :width]),
        (g_ref, qg_ref.at[:, width:]),
        (plan_ref, plan_out),
    )
    copies = [pltpu.make_async_copy(a, b, sems.at[i]) for i, (a, b) in enumerate(moves)]
    for copy in copies:
        copy.start()
    for copy in copies[:2]:
        copy.wait()

    @pl.when(side == 0)
    def _():
        half_ref[...] = kv_ref[:, :dim]

    @pl.when(side == 1)
    def _():
        half_ref[...] = kv_ref[:, dim:]

    for copy in copies[2:]:
        copy.wait()


def loop(count, body, carry):
    if count <= 8:
        for j in range(count):
            carry = body(j, carry)
        return carry
    return lax.fori_loop(0, count, body, carry)

def rows_at(c):
    start = c * CHUNK
    return pl.ds(start if isinstance(start, int) else pl.multiple_of(start, CHUNK), CHUNK)


def contract(sizes, low, buf, ref, i):
    rounds, reach, tok, heads, head_dim = sizes
    lanes = heads * CHUNK
    span = 2 * reach + 2
    slot = slice(i * lanes, (i + 1) * lanes)
    if span <= 8:
        rows = (2 * reach + 1) * CHUNK
        at = pl.ds(pl.multiple_of((low + i) * CHUNK, CHUNK), rows)
        return tn(buf[at, :], ref[i * CHUNK:i * CHUNK + rows, slot])

    def add(j, acc):
        return acc + tn(buf[rows_at(low + j), :], ref[rows_at(j), slot])

    return lax.fori_loop(0, span, add, jnp.zeros((head_dim, lanes), jnp.float32))


def two_stretches(sizes, begin_ref, z, column, kbuf, vbuf, q_all, g_all, w_ref, p_ref, d_ref,
                  od_ref, blocks, put):
    rounds, reach, tok, heads, head_dim = sizes
    inv_root = 1.0 / math.sqrt(head_dim)
    width = heads * head_dim
    lanes = heads * CHUNK
    span = 2 * reach + 2
    unrolled = span <= 8
    low = 4 * rounds + 2 * column - 2 * reach
    low_place = (2 * (z - rounds) * tok) + low * CHUNK
    q, g, places, begin = [], [], [], []
    for i in range(2):
        rows = slice(i * CHUNK, (i + 1) * CHUNK)
        q.append(jnp.concatenate(
            [q_all[rows, h * head_dim:(h + 1) * head_dim] for h in range(heads)], axis=0))
        g.append(jnp.concatenate(
            [g_all[rows, h * head_dim:(h + 1) * head_dim] for h in range(heads)], axis=0))
        lane = lax.broadcasted_iota(jnp.int32, (1, lanes), 1) % CHUNK
        place = (2 * z + column) * tok + i * CHUNK + lane
        places.append(place)
        begin.append(begin_ref[i:i + 1, :])

    def slots(j):
        if not unrolled:
            return (0, 1)
        return tuple(i for i in range(2) if i <= j <= 2 * reach + i)

    def scores(j, tops):
        tops = list(tops)
        k = kbuf[rows_at(low + j), :]
        at = low_place + j * CHUNK + lax.broadcasted_iota(jnp.int32, (CHUNK, lanes), 0)
        for i in slots(j):
            allowed = at >= begin[i]
            if not unrolled or j == 2 * reach + i:
                allowed = allowed & (at <= places[i])
            s = jnp.where(allowed, nt(k, q[i]) * (inv_root * LOG2E), NEG)
            w_ref[i, j] = s
            tops[i] = jnp.maximum(tops[i], fold(s, jnp.max))
        return tuple(tops)

    full = lambda value: tuple(jnp.full((8, lanes), value, jnp.float32) for _ in range(2))
    tops = loop(span, scores, full(NEG))
    tops = [jnp.max(t, axis=0, keepdims=True) for t in tops]

    def exps(j, totals):
        totals = list(totals)
        for i in slots(j):
            e = jnp.exp2(w_ref[i, j] - tops[i])
            w_ref[i, j] = e
            p_ref[rows_at(j), slice(i * lanes, (i + 1) * lanes)] = e.astype(jnp.bfloat16)
            totals[i] = totals[i] + fold(e, jnp.sum)
        return tuple(totals)

    totals = loop(span, exps, full(0.0))
    scale = [1.0 / jnp.sum(t, axis=0, keepdims=True) for t in totals]
    dots = []
    for i in range(2):
        attended = (contract(sizes, low, vbuf, p_ref, i) * scale[i]).T.astype(jnp.bfloat16)
        for h in range(heads):
            od_ref[i * CHUNK:(i + 1) * CHUNK, h * head_dim:(h + 1) * head_dim] = (
                attended[h * CHUNK:(h + 1) * CHUNK])
        product = g[i].astype(jnp.float32) * attended.astype(jnp.float32)
        dots.append(jnp.sum(product.T, axis=0, keepdims=True))

    def backward(j, carry):
        v = vbuf[rows_at(low + j), :]
        for i in range(2):
            if i in slots(j):
                w = w_ref[i, j] * scale[i]
                ds = (w * (nt(v, g[i]) - dots[i])).astype(jnp.bfloat16)
                d_ref[rows_at(j), slice(i * lanes, (i + 1) * lanes)] = ds
                p_ref[rows_at(j), slice(i * lanes, (i + 1) * lanes)] = w.astype(jnp.bfloat16)
            else:
                blank = jnp.zeros((CHUNK, lanes), jnp.bfloat16)
                d_ref[rows_at(j), slice(i * lanes, (i + 1) * lanes)] = blank
                p_ref[rows_at(j), slice(i * lanes, (i + 1) * lanes)] = blank
        return carry

    loop(span, backward, 0)
    q_both = jnp.concatenate(q, axis=0)
    g_both = jnp.concatenate(g, axis=0)

    def keys(m, carry):
        first, count = blocks
        b = first + 2 * m
        start = b * tok
        at = pl.ds(start if isinstance(start, int) else pl.multiple_of(start, tok), tok)
        put(count - 1 - m, nn(d_ref[at, :], q_both) * inv_root, nn(p_ref[at, :], g_both))
        return carry

    loop(blocks[1], keys, 0)


def query_grads(sizes, column, kbuf, d_ref, od_ref):
    rounds, reach, tok, heads, head_dim = sizes
    inv_root = 1.0 / math.sqrt(head_dim)
    low = 4 * rounds + 2 * column - 2 * reach
    width = heads * head_dim
    for i in range(2):
        grad = (contract(sizes, low, kbuf, d_ref, i) * inv_root).T.astype(jnp.bfloat16)
        for h in range(heads):
            at = width + h * head_dim
            od_ref[i * CHUNK:(i + 1) * CHUNK, at:at + head_dim] = (
                grad[h * CHUNK:(h + 1) * CHUNK])


def own_kernel(sizes):
    rounds, reach, tok, heads, head_dim = sizes

    def kernel(begin_ref, k_ref, v_ref, q_ref, g_ref, mine_ref, other_ref, half_ref, cross_ref,
               att_ref, d_ref, kv_out, kbuf, vbuf, w_ref, p_ref):
        here = lax.axis_index("ctx")
        side = lax.axis_index("head")
        z = here // 2
        x = here % 2

        for r in range(rounds):
            for ref, column in ((mine_ref, (x + side) % 2), (other_ref, (x + 1 - side) % 2)):
                at = pl.ds(pl.multiple_of((2 * (rounds - 1 - r) + column) * tok, tok), tok)
                kbuf[at, :] = ref[r, :, :head_dim]
                vbuf[at, :] = ref[r, :, head_dim:]
        own = pl.ds(pl.multiple_of((2 * rounds + x) * tok, tok), tok)
        kbuf[own, :] = k_ref[...]
        vbuf[own, :] = v_ref[...]
        next_to = pl.ds(pl.multiple_of((2 * rounds + 1 - x) * tok, tok), tok)

        @pl.when(side == 0)
        def _():
            kbuf[next_to, :] = half_ref[...]
            vbuf[next_to, :] = cross_ref[...]

        @pl.when(side == 1)
        def _():
            vbuf[next_to, :] = half_ref[...]
            kbuf[next_to, :] = cross_ref[...]

        def put(r, dk, dv):
            kv_out[r, :, :head_dim] = dk
            kv_out[r, :, head_dim:] = dv

        two_stretches(sizes, begin_ref, z, x, kbuf, vbuf, q_ref, g_ref, w_ref, p_ref, d_ref,
                      att_ref, (0, rounds + 1), put)

    return kernel


def next_kernel(sizes):
    rounds, reach, tok, heads, head_dim = sizes
    width = heads * head_dim

    def kernel(begin_ref, kbuf, vbuf, qg_ref, own_kv, att_ref, d_ref, kv_out, far_out,
               w_ref, p_ref, sums):
        here = lax.axis_index("ctx")
        z = here // 2
        x = here % 2
        sums[...] = own_kv[...]

        def put(r, dk, dv):
            at = r + x
            sums[at, :, :head_dim] = sums[at, :, :head_dim] + dk
            sums[at, :, head_dim:] = sums[at, :, head_dim:] + dv

        two_stretches(sizes, begin_ref, z, 1 - x, kbuf, vbuf, qg_ref.at[:, :width],
                      qg_ref.at[:, width:], w_ref, p_ref, d_ref, att_ref, (1, rounds), put)
        kv_out[...] = sums[0]
        far_out[...] = sums[1:].astype(far_out.dtype)

    return kernel


def send_kernel(sizes):
    rounds, reach, tok, heads, head_dim = sizes
    width = heads * head_dim

    def kernel(plan_ref, kbuf, d_own, d_next, att_own, att_next, od_ref, send_a, send_b):
        here = lax.axis_index("ctx")
        side = lax.axis_index("head")
        x = here % 2
        plan = scalars(plan_ref, 4)
        for at, column, att, d_ref in ((0, x, att_own, d_own), (tok, 1 - x, att_next, d_next)):
            rows = od_ref.at[at:at + tok, :]
            rows[:, :width] = att[...]
            query_grads(sizes, column, kbuf, d_ref, rows)
        for way, out in enumerate((send_a, send_b)):
            flip = (side + way) % 2
            for i in range(2):
                wanted = jnp.where(flip == 0, plan[i], plan[2 + i])
                out[i * CHUNK:(i + 1) * CHUNK, :] = od_ref[row_of(wanted, x), :]

    return kernel


def row_of(wanted, x):
    inner = wanted % 4
    return pl.ds(pl.multiple_of(((inner + 2 * x) % 4) * CHUNK, CHUNK), CHUNK)


def place_kernel(width):
    def kernel(plan_ref, row_ref, a_ref, b_ref, s_ref, t_ref, out_ref, dq_ref, dk_ref, dv_ref):
        here = lax.axis_index("ctx")
        side = lax.axis_index("head")
        z = here // 2
        source_a = up_down(z, side)
        plan = scalars(plan_ref, 2)
        for slot in range(2):
            wanted = plan[slot]
            to = pl.ds(slot * CHUNK, CHUNK)
            inside = row_of(wanted, here % 2)

            def put(rows):
                out_ref[to, :] = rows[:, :width]
                dq_ref[to, :] = rows[:, width:].astype(jnp.float32)

            home = wanted // 4 == z
            from_a = wanted // 4 == source_a
            pl.when(home)(lambda: put(row_ref[inside, :]))
            pl.when(from_a)(lambda: put(a_ref[to, :]))
            pl.when(jnp.logical_not(home | from_a))(lambda: put(b_ref[to, :]))
        half = dk_ref.shape[1]
        dk_ref[...] = s_ref[:, :half] + t_ref[:, :half]
        dv_ref[...] = s_ref[:, half:] + t_ref[:, half:]

    return kernel


def per_device(queries, key_input, value_input, grad_out, doc_lengths, stretch_plan):
    tok, head_dim = key_input.shape
    width = queries.shape[1]
    heads = width // head_dim
    n = lax.axis_size("ctx")
    rounds = (min(DOC_CAP, tok * n // 4) // tok + 1) // 2
    reach = 2 * rounds
    bf16, f32 = jnp.bfloat16, jnp.float32
    both = ("ctx", "head")
    cross = [(0, 1), (1, 0)]
    side = lax.axis_index("head")

    here = lax.axis_index("ctx")
    order = jnp.arange(doc_lengths.shape[0], dtype=jnp.int32)
    bounds = jnp.sum(jnp.where(order[None, :] <= order[:, None], doc_lengths[None, :], 0), axis=1)

    def begins(device):
        places = device * tok + jnp.arange(tok, dtype=jnp.int32)
        starts = jnp.max(jnp.where(bounds[:, None] <= places[None, :], bounds[:, None], 0), axis=0)
        starts = starts.reshape(tok // CHUNK, 1, CHUNK)
        return jnp.broadcast_to(starts, (tok // CHUNK, heads, CHUNK)).reshape(tok // CHUNK, -1)

    def lanes_of(values):
        return jnp.pad(values, (0, 128 - values.shape[0])).reshape(1, 128)

    def fetch_pairs(r):
        pairs = []
        for s in range(n):
            for h in range(2):
                to = s // 2 + r + 1
                column = (s + h) % 2 if to < n // 2 else s % 2
                pairs.append((2 * s + h, 2 * (2 * (to % (n // 2)) + column) + h))
        return pairs

    def back_pairs(r):
        return [(s, s - 2 * r) for s in range(2 * r, n)]

    plan_out, own_kv, half, queries_grads = pl.pallas_call(
        pack_kernel,
        out_shape=(
            pltpu.VMEM(stretch_plan.shape, jnp.int32),
            pltpu.VMEM((tok, 2 * head_dim), bf16),
            pltpu.VMEM((tok, head_dim), bf16),
            pltpu.VMEM((tok, 2 * width), bf16),
        ),
        in_specs=[pl.BlockSpec(memory_space=pl.ANY)] * 5,
        out_specs=(VMEM,) * 4,
        scratch_shapes=[pltpu.SemaphoreType.DMA((5,))],
        name="pack",
    )(stretch_plan, key_input, value_input, queries, grad_out)
    tie_a, tie_b = row_pairs(n // 2)
    near = [(i, i ^ 1) for i in range(n)]
    part = lax.ppermute(queries_grads, "ctx", near)
    half_next = lax.ppermute(half, "ctx", near)
    mine = [lax.ppermute(own_kv, both, fetch_pairs(r)) for r in range(rounds)]
    mine = jnp.stack(mine)
    other = lax.ppermute(mine, "head", cross)
    half_cross = lax.ppermute(half_next, "head", cross)
    sizes = (rounds, reach, tok, heads, head_dim)
    params = pltpu.CompilerParams(vmem_limit_bytes=40 << 20)
    span = 2 * reach + 2
    weights = pltpu.VMEM((span * CHUNK, 2 * heads * CHUNK), bf16)
    scores = pltpu.VMEM((2, span, CHUNK, heads * CHUNK), f32)
    buffer = jax.ShapeDtypeStruct(((2 * rounds + 2) * tok, head_dim), bf16)
    rows = jax.ShapeDtypeStruct((tok, 2 * width), bf16)
    attended = jax.ShapeDtypeStruct((tok, width), bf16)
    grads = jax.ShapeDtypeStruct((span * CHUNK, 2 * heads * CHUNK), bf16)
    key_sums = jax.ShapeDtypeStruct((rounds + 1, tok, 2 * head_dim), f32)
    att_own, d_own, kv_own, kbuf, vbuf = pl.pallas_call(
        own_kernel(sizes),
        out_shape=(attended, grads, key_sums, buffer, buffer),
        in_specs=[VMEM] * 9,
        out_specs=(VMEM,) * 5,
        scratch_shapes=[scores, weights],
        compiler_params=params,
        name="attend_own",
    )(begins(here), key_input, value_input, queries, grad_out, mine, other, half_next,
      half_cross)
    kv_own, stretch_here = lax.optimization_barrier((kv_own, plan_out))
    plan_mine = lax.ppermute(stretch_here, both, tie_a)
    plan_other = lax.ppermute(plan_mine, "head", cross)
    plans = jnp.where(side == 0, jnp.concatenate([plan_mine, plan_other]),
                      jnp.concatenate([plan_other, plan_mine]))
    att_next, d_next, kv_sum, far = pl.pallas_call(
        next_kernel(sizes),
        out_shape=(
            attended, grads, jax.ShapeDtypeStruct((tok, 2 * head_dim), f32),
            jax.ShapeDtypeStruct((rounds, tok, 2 * head_dim), bf16),
        ),
        in_specs=[VMEM] * 5,
        out_specs=(VMEM,) * 4,
        scratch_shapes=[scores, weights, pltpu.VMEM((rounds + 1, tok, 2 * head_dim), f32)],
        compiler_params=params,
        name="attend_next",
    )(begins(here ^ 1), kbuf, vbuf, part, kv_own)
    od, send_a, send_b = pl.pallas_call(
        send_kernel(sizes),
        out_shape=(jax.ShapeDtypeStruct((2 * tok, 2 * width), bf16), rows, rows),
        in_specs=[VMEM] * 6,
        out_specs=(VMEM,) * 3,
        compiler_params=params,
        name="send_rows",
    )(lanes_of(plans), kbuf, d_own, d_next, att_own, att_next)

    moved_a = lax.ppermute(send_a, both, tie_a)
    moved_b = lax.ppermute(send_b, both, tie_b)
    total = kv_sum
    for r in range(rounds):
        total = total + lax.ppermute(far[r], "ctx", back_pairs(r + 1)).astype(f32)
    total_other = lax.ppermute(total, "head", cross)

    output, query_grad, key_grad, value_grad = pl.pallas_call(
        place_kernel(width),
        out_shape=(
            jax.ShapeDtypeStruct((tok, width), bf16),
            jax.ShapeDtypeStruct((tok, width), f32),
            jax.ShapeDtypeStruct((tok, head_dim), f32),
            jax.ShapeDtypeStruct((tok, head_dim), f32),
        ),
        in_specs=[VMEM] * 6,
        out_specs=(VMEM,) * 4,
        compiler_params=pltpu.CompilerParams(vmem_limit_bytes=32 << 20),
        name="place",
    )(lanes_of(stretch_plan), od, moved_a, moved_b, total, total_other)
    return (output, query_grad, key_grad, value_grad)


def solution(mesh):
    return jax.shard_map(
        per_device,
        mesh=mesh,
        in_specs=(
            P(("groups", "ctx"), "head"),
            P(("groups", "ctx"), None),
            P(("groups", "ctx"), None),
            P(("groups", "ctx"), "head"),
            P("groups"),
            P(("groups", "ctx")),
        ),
        out_specs=(
            P(("groups", "ctx"), "head"),
            P(("groups", "ctx"), "head"),
            P(("groups", "ctx"), None),
            P(("groups", "ctx"), None),
        ),
        check_vma=False,
    )
```

```python
import math

import jax
import jax.numpy as jnp
from jax import lax
from jax.experimental import pallas as pl
from jax.experimental.pallas import tpu as pltpu
from jax.sharding import PartitionSpec as P

DOC_CAP = 4096
NEG = -1e30


LOG2E = 1.4426950408889634
CHUNK = 128

VMEM = pl.BlockSpec(memory_space=pltpu.VMEM)
SMEM = pl.BlockSpec(memory_space=pltpu.SMEM)


def nt(a, b):
    return lax.dot_general(a, b, (((1,), (1,)), ((), ())), preferred_element_type=jnp.float32)


def nn(a, b):
    return lax.dot_general(a, b, (((1,), (0,)), ((), ())), preferred_element_type=jnp.float32)


def tn(a, b):
    return lax.dot_general(a, b, (((0,), (0,)), ((), ())), preferred_element_type=jnp.float32)


def fold(a, op):
    rows = a.shape[0] // 8
    parts = a.reshape(rows, 8, a.shape[1])
    return op(parts, axis=0)


def scalars(ref, count):
    row = ref[...]
    lane = lax.broadcasted_iota(jnp.int32, row.shape, 1)
    return [jnp.sum(jnp.where(lane == i, row, 0)) for i in range(count)]


def up_down(z, flip):
    return z + 1 - 2 * ((z + flip) % 2)


def row_pairs(rows):
    pairs = ([], [])
    for z in range(rows):
        for x in range(2):
            for h in range(2):
                for way in range(2):
                    to = z + 1 - 2 * ((z + (h ^ way)) % 2)
                    other = (to, x) if 0 <= to < rows else (z, 1 - x)
                    node = 4 * z + 2 * x + h
                    pairs[way].append((node, 4 * other[0] + 2 * other[1] + h))
    return pairs


def pack_kernel(plan_ref, k_ref, v_ref, q_ref, g_ref, plan_out, kv_ref, half_ref, qg_ref, sems):
    side = lax.axis_index("head")
    dim = k_ref.shape[1]
    width = q_ref.shape[1]
    moves = (
        (k_ref, kv_ref.at[:, :dim]),
        (v_ref, kv_ref.at[:, dim:]),
        (q_ref, qg_ref.at[:, :width]),
        (g_ref, qg_ref.at[:, width:]),
        (plan_ref, plan_out),
    )
    copies = [pltpu.make_async_copy(a, b, sems.at[i]) for i, (a, b) in enumerate(moves)]
    for copy in copies:
        copy.start()
    for copy in copies[:2]:
        copy.wait()

    @pl.when(side == 0)
    def _():
        half_ref[...] = kv_ref[:, :dim]

    @pl.when(side == 1)
    def _():
        half_ref[...] = kv_ref[:, dim:]

    for copy in copies[2:]:
        copy.wait()


def loop(count, body, carry):
    if count <= 8:
        for j in range(count):
            carry = body(j, carry)
        return carry
    return lax.fori_loop(0, count, body, carry)

def rows_at(c):
    start = c * CHUNK
    return pl.ds(start if isinstance(start, int) else pl.multiple_of(start, CHUNK), CHUNK)


def contract(sizes, low, buf, ref, i):
    rounds, reach, tok, heads, head_dim = sizes
    lanes = heads * CHUNK
    span = 2 * reach + 2
    slot = slice(i * lanes, (i + 1) * lanes)
    if span <= 8:
        rows = (2 * reach + 1) * CHUNK
        at = pl.ds(pl.multiple_of((low + i) * CHUNK, CHUNK), rows)
        return tn(buf[at, :], ref[i * CHUNK:i * CHUNK + rows, slot])

    def add(j, acc):
        return acc + tn(buf[rows_at(low + j), :], ref[rows_at(j), slot])

    return lax.fori_loop(0, span, add, jnp.zeros((head_dim, lanes), jnp.float32))


def two_stretches(sizes, begin_ref, z, column, kbuf, vbuf, q_all, g_all, w_ref, p_ref, d_ref,
                  od_ref, blocks, put):
    rounds, reach, tok, heads, head_dim = sizes
    inv_root = 1.0 / math.sqrt(head_dim)
    width = heads * head_dim
    lanes = heads * CHUNK
    span = 2 * reach + 2
    unrolled = span <= 8
    low = 4 * rounds + 2 * column - 2 * reach
    low_place = (2 * (z - rounds) * tok) + low * CHUNK
    q, g, places, begin = [], [], [], []
    for i in range(2):
        rows = slice(i * CHUNK, (i + 1) * CHUNK)
        q.append(jnp.concatenate(
            [q_all[rows, h * head_dim:(h + 1) * head_dim] for h in range(heads)], axis=0))
        g.append(jnp.concatenate(
            [g_all[rows, h * head_dim:(h + 1) * head_dim] for h in range(heads)], axis=0))
        lane = lax.broadcasted_iota(jnp.int32, (1, lanes), 1) % CHUNK
        place = (2 * z + column) * tok + i * CHUNK + lane
        places.append(place)
        begin.append(begin_ref[i:i + 1, :])

    def slots(j):
        if not unrolled:
            return (0, 1)
        return tuple(i for i in range(2) if i <= j <= 2 * reach + i)

    def scores(j, tops):
        tops = list(tops)
        k = kbuf[rows_at(low + j), :]
        at = low_place + j * CHUNK + lax.broadcasted_iota(jnp.int32, (CHUNK, lanes), 0)
        for i in slots(j):
            allowed = at >= begin[i]
            if not unrolled or j == 2 * reach + i:
                allowed = allowed & (at <= places[i])
            s = jnp.where(allowed, nt(k, q[i]) * (inv_root * LOG2E), NEG)
            w_ref[i, j] = s
            tops[i] = jnp.maximum(tops[i], fold(s, jnp.max))
        return tuple(tops)

    full = lambda value: tuple(jnp.full((8, lanes), value, jnp.float32) for _ in range(2))
    tops = loop(span, scores, full(NEG))
    tops = [jnp.max(t, axis=0, keepdims=True) for t in tops]

    def exps(j, totals):
        totals = list(totals)
        for i in slots(j):
            e = jnp.exp2(w_ref[i, j] - tops[i])
            w_ref[i, j] = e
            p_ref[rows_at(j), slice(i * lanes, (i + 1) * lanes)] = e.astype(jnp.bfloat16)
            totals[i] = totals[i] + fold(e, jnp.sum)
        return tuple(totals)

    totals = loop(span, exps, full(0.0))
    scale = [1.0 / jnp.sum(t, axis=0, keepdims=True) for t in totals]
    dots = []
    for i in range(2):
        total = contract(sizes, low, vbuf, p_ref, i) * scale[i]
        attended = total.T.astype(jnp.bfloat16)
        for h in range(heads):
            od_ref[i * CHUNK:(i + 1) * CHUNK, h * head_dim:(h + 1) * head_dim] = (
                attended[h * CHUNK:(h + 1) * CHUNK])
        rounded = total.astype(jnp.bfloat16).astype(jnp.float32)
        dots.append(jnp.sum(g[i].astype(jnp.float32).T * rounded, axis=0, keepdims=True))

    def backward(j, carry):
        v = vbuf[rows_at(low + j), :]
        for i in range(2):
            if i in slots(j):
                w = w_ref[i, j] * scale[i]
                ds = (w * (nt(v, g[i]) - dots[i])).astype(jnp.bfloat16)
                d_ref[rows_at(j), slice(i * lanes, (i + 1) * lanes)] = ds
                p_ref[rows_at(j), slice(i * lanes, (i + 1) * lanes)] = w.astype(jnp.bfloat16)
            else:
                blank = jnp.zeros((CHUNK, lanes), jnp.bfloat16)
                d_ref[rows_at(j), slice(i * lanes, (i + 1) * lanes)] = blank
                p_ref[rows_at(j), slice(i * lanes, (i + 1) * lanes)] = blank
        return carry

    loop(span, backward, 0)
    q_both = jnp.concatenate(q, axis=0)
    g_both = jnp.concatenate(g, axis=0)

    def keys(m, carry):
        first, count = blocks
        b = first + 2 * m
        start = b * tok
        at = pl.ds(start if isinstance(start, int) else pl.multiple_of(start, tok), tok)
        put(count - 1 - m, nn(d_ref[at, :], q_both) * inv_root, nn(p_ref[at, :], g_both))
        return carry

    loop(blocks[1], keys, 0)


def query_grads(sizes, column, kbuf, d_ref, od_ref):
    rounds, reach, tok, heads, head_dim = sizes
    inv_root = 1.0 / math.sqrt(head_dim)
    low = 4 * rounds + 2 * column - 2 * reach
    width = heads * head_dim
    for i in range(2):
        grad = (contract(sizes, low, kbuf, d_ref, i) * inv_root).T.astype(jnp.bfloat16)
        for h in range(heads):
            at = width + h * head_dim
            od_ref[i * CHUNK:(i + 1) * CHUNK, at:at + head_dim] = (
                grad[h * CHUNK:(h + 1) * CHUNK])


def own_kernel(sizes):
    rounds, reach, tok, heads, head_dim = sizes

    def kernel(begin_ref, k_ref, v_ref, q_ref, g_ref, mine_ref, other_ref, half_ref, cross_ref,
               att_ref, d_ref, kv_out, kbuf, vbuf, w_ref, p_ref):
        here = lax.axis_index("ctx")
        side = lax.axis_index("head")
        z = here // 2
        x = here % 2

        for r in range(rounds):
            for ref, column in ((mine_ref, (x + side) % 2), (other_ref, (x + 1 - side) % 2)):
                at = pl.ds(pl.multiple_of((2 * (rounds - 1 - r) + column) * tok, tok), tok)
                kbuf[at, :] = ref[r, :, :head_dim]
                vbuf[at, :] = ref[r, :, head_dim:]
        own = pl.ds(pl.multiple_of((2 * rounds + x) * tok, tok), tok)
        kbuf[own, :] = k_ref[...]
        vbuf[own, :] = v_ref[...]
        next_to = pl.ds(pl.multiple_of((2 * rounds + 1 - x) * tok, tok), tok)

        @pl.when(side == 0)
        def _():
            kbuf[next_to, :] = half_ref[...]
            vbuf[next_to, :] = cross_ref[...]

        @pl.when(side == 1)
        def _():
            vbuf[next_to, :] = half_ref[...]
            kbuf[next_to, :] = cross_ref[...]

        def put(r, dk, dv):
            kv_out[r, :, :head_dim] = dk
            kv_out[r, :, head_dim:] = dv

        two_stretches(sizes, begin_ref, z, x, kbuf, vbuf, q_ref, g_ref, w_ref, p_ref, d_ref,
                      att_ref, (0, rounds + 1), put)

    return kernel


def next_kernel(sizes):
    rounds, reach, tok, heads, head_dim = sizes
    width = heads * head_dim

    def kernel(begin_ref, kbuf, vbuf, qg_ref, own_kv, att_ref, d_ref, kv_out, far_out,
               w_ref, p_ref, sums):
        here = lax.axis_index("ctx")
        z = here // 2
        x = here % 2
        sums[...] = own_kv[...]

        def put(r, dk, dv):
            at = r + x
            sums[at, :, :head_dim] = sums[at, :, :head_dim] + dk
            sums[at, :, head_dim:] = sums[at, :, head_dim:] + dv

        two_stretches(sizes, begin_ref, z, 1 - x, kbuf, vbuf, qg_ref.at[:, :width],
                      qg_ref.at[:, width:], w_ref, p_ref, d_ref, att_ref, (1, rounds), put)
        kv_out[...] = sums[0]
        far_out[...] = sums[1:].astype(far_out.dtype)

    return kernel


def send_kernel(sizes):
    rounds, reach, tok, heads, head_dim = sizes
    width = heads * head_dim

    def kernel(plan_ref, kbuf, d_own, d_next, att_own, att_next, od_ref, send_a, send_b):
        here = lax.axis_index("ctx")
        side = lax.axis_index("head")
        x = here % 2
        plan = scalars(plan_ref, 4)
        for at, column, att, d_ref in ((0, x, att_own, d_own), (tok, 1 - x, att_next, d_next)):
            rows = od_ref.at[at:at + tok, :]
            rows[:, :width] = att[...]
            query_grads(sizes, column, kbuf, d_ref, rows)
        for way, out in enumerate((send_a, send_b)):
            flip = (side + way) % 2
            for i in range(2):
                wanted = jnp.where(flip == 0, plan[i], plan[2 + i])
                out[i * CHUNK:(i + 1) * CHUNK, :] = od_ref[row_of(wanted, x), :]

    return kernel


def row_of(wanted, x):
    inner = wanted % 4
    return pl.ds(pl.multiple_of(((inner + 2 * x) % 4) * CHUNK, CHUNK), CHUNK)


def place_kernel(width):
    def kernel(plan_ref, row_ref, a_ref, b_ref, s_ref, t_ref, out_ref, dq_ref, dk_ref, dv_ref):
        here = lax.axis_index("ctx")
        side = lax.axis_index("head")
        z = here // 2
        source_a = up_down(z, side)
        plan = scalars(plan_ref, 2)
        for slot in range(2):
            wanted = plan[slot]
            to = pl.ds(slot * CHUNK, CHUNK)
            inside = row_of(wanted, here % 2)

            def put(rows):
                out_ref[to, :] = rows[:, :width]
                dq_ref[to, :] = rows[:, width:].astype(jnp.float32)

            home = wanted // 4 == z
            from_a = wanted // 4 == source_a
            pl.when(home)(lambda: put(row_ref[inside, :]))
            pl.when(from_a)(lambda: put(a_ref[to, :]))
            pl.when(jnp.logical_not(home | from_a))(lambda: put(b_ref[to, :]))
        half = dk_ref.shape[1]
        dk_ref[...] = s_ref[:, :half] + t_ref[:, :half]
        dv_ref[...] = s_ref[:, half:] + t_ref[:, half:]

    return kernel


def per_device(queries, key_input, value_input, grad_out, doc_lengths, stretch_plan):
    tok, head_dim = key_input.shape
    width = queries.shape[1]
    heads = width // head_dim
    n = lax.axis_size("ctx")
    rounds = (min(DOC_CAP, tok * n // 4) // tok + 1) // 2
    reach = 2 * rounds
    bf16, f32 = jnp.bfloat16, jnp.float32
    both = ("ctx", "head")
    cross = [(0, 1), (1, 0)]
    side = lax.axis_index("head")

    here = lax.axis_index("ctx")
    order = jnp.arange(doc_lengths.shape[0], dtype=jnp.int32)
    bounds = jnp.sum(jnp.where(order[None, :] <= order[:, None], doc_lengths[None, :], 0), axis=1)

    def begins(device):
        places = device * tok + jnp.arange(tok, dtype=jnp.int32)
        starts = jnp.max(jnp.where(bounds[:, None] <= places[None, :], bounds[:, None], 0), axis=0)
        starts = starts.reshape(tok // CHUNK, 1, CHUNK)
        return jnp.broadcast_to(starts, (tok // CHUNK, heads, CHUNK)).reshape(tok // CHUNK, -1)

    def lanes_of(values):
        return jnp.pad(values, (0, 128 - values.shape[0])).reshape(1, 128)

    def fetch_pairs(r):
        pairs = []
        for s in range(n):
            for h in range(2):
                to = s // 2 + r + 1
                column = (s + h) % 2 if to < n // 2 else s % 2
                pairs.append((2 * s + h, 2 * (2 * (to % (n // 2)) + column) + h))
        return pairs

    def back_pairs(r):
        return [(s, s - 2 * r) for s in range(2 * r, n)]

    plan_out, own_kv, half, queries_grads = pl.pallas_call(
        pack_kernel,
        out_shape=(
            pltpu.VMEM(stretch_plan.shape, jnp.int32),
            pltpu.VMEM((tok, 2 * head_dim), bf16),
            pltpu.VMEM((tok, head_dim), bf16),
            pltpu.VMEM((tok, 2 * width), bf16),
        ),
        in_specs=[pl.BlockSpec(memory_space=pl.ANY)] * 5,
        out_specs=(VMEM,) * 4,
        scratch_shapes=[pltpu.SemaphoreType.DMA((5,))],
        name="pack",
    )(stretch_plan, key_input, value_input, queries, grad_out)
    tie_a, tie_b = row_pairs(n // 2)
    near = [(i, i ^ 1) for i in range(n)]
    part = lax.ppermute(queries_grads, "ctx", near)
    half_next = lax.ppermute(half, "ctx", near)
    mine = [lax.ppermute(own_kv, both, fetch_pairs(r)) for r in range(rounds)]
    mine = jnp.stack(mine)
    other = lax.ppermute(mine, "head", cross)
    half_cross = lax.ppermute(half_next, "head", cross)
    sizes = (rounds, reach, tok, heads, head_dim)
    params = pltpu.CompilerParams(vmem_limit_bytes=40 << 20)
    span = 2 * reach + 2
    weights = pltpu.VMEM((span * CHUNK, 2 * heads * CHUNK), bf16)
    scores = pltpu.VMEM((2, span, CHUNK, heads * CHUNK), f32)
    buffer = jax.ShapeDtypeStruct(((2 * rounds + 2) * tok, head_dim), bf16)
    rows = jax.ShapeDtypeStruct((tok, 2 * width), bf16)
    attended = jax.ShapeDtypeStruct((tok, width), bf16)
    grads = jax.ShapeDtypeStruct((span * CHUNK, 2 * heads * CHUNK), bf16)
    key_sums = jax.ShapeDtypeStruct((rounds + 1, tok, 2 * head_dim), f32)
    att_own, d_own, kv_own, kbuf, vbuf = pl.pallas_call(
        own_kernel(sizes),
        out_shape=(attended, grads, key_sums, buffer, buffer),
        in_specs=[VMEM] * 9,
        out_specs=(VMEM,) * 5,
        scratch_shapes=[scores, weights],
        compiler_params=params,
        name="attend_own",
    )(begins(here), key_input, value_input, queries, grad_out, mine, other, half_next,
      half_cross)
    kv_own, stretch_here = lax.optimization_barrier((kv_own, plan_out))
    plan_mine = lax.ppermute(stretch_here, both, tie_a)
    plan_other = lax.ppermute(plan_mine, "head", cross)
    plans = jnp.where(side == 0, jnp.concatenate([plan_mine, plan_other]),
                      jnp.concatenate([plan_other, plan_mine]))
    att_next, d_next, kv_sum, far = pl.pallas_call(
        next_kernel(sizes),
        out_shape=(
            attended, grads, jax.ShapeDtypeStruct((tok, 2 * head_dim), f32),
            jax.ShapeDtypeStruct((rounds, tok, 2 * head_dim), bf16),
        ),
        in_specs=[VMEM] * 5,
        out_specs=(VMEM,) * 4,
        scratch_shapes=[scores, weights, pltpu.VMEM((rounds + 1, tok, 2 * head_dim), f32)],
        compiler_params=params,
        name="attend_next",
    )(begins(here ^ 1), kbuf, vbuf, part, kv_own)
    od, send_a, send_b = pl.pallas_call(
        send_kernel(sizes),
        out_shape=(jax.ShapeDtypeStruct((2 * tok, 2 * width), bf16), rows, rows),
        in_specs=[VMEM] * 6,
        out_specs=(VMEM,) * 3,
        compiler_params=params,
        name="send_rows",
    )(lanes_of(plans), kbuf, d_own, d_next, att_own, att_next)

    moved_a = lax.ppermute(send_a, both, tie_a)
    moved_b = lax.ppermute(send_b, both, tie_b)
    total = kv_sum
    for r in range(rounds):
        total = total + lax.ppermute(far[r], "ctx", back_pairs(r + 1)).astype(f32)
    total_other = lax.ppermute(total, "head", cross)

    output, query_grad, key_grad, value_grad = pl.pallas_call(
        place_kernel(width),
        out_shape=(
            jax.ShapeDtypeStruct((tok, width), bf16),
            jax.ShapeDtypeStruct((tok, width), f32),
            jax.ShapeDtypeStruct((tok, head_dim), f32),
            jax.ShapeDtypeStruct((tok, head_dim), f32),
        ),
        in_specs=[VMEM] * 6,
        out_specs=(VMEM,) * 4,
        compiler_params=pltpu.CompilerParams(vmem_limit_bytes=32 << 20),
        name="place",
    )(lanes_of(stretch_plan), od, moved_a, moved_b, total, total_other)
    return (output, query_grad, key_grad, value_grad)


def solution(mesh):
    return jax.shard_map(
        per_device,
        mesh=mesh,
        in_specs=(
            P(("groups", "ctx"), "head"),
            P(("groups", "ctx"), None),
            P(("groups", "ctx"), None),
            P(("groups", "ctx"), "head"),
            P("groups"),
            P(("groups", "ctx")),
        ),
        out_specs=(
            P(("groups", "ctx"), "head"),
            P(("groups", "ctx"), "head"),
            P(("groups", "ctx"), None),
            P(("groups", "ctx"), None),
        ),
        check_vma=False,
    )
```

```python
import math

import jax
import jax.numpy as jnp
from jax import lax
from jax.experimental import pallas as pl
from jax.experimental.pallas import tpu as pltpu
from jax.sharding import PartitionSpec as P

DOC_CAP = 4096
NEG = -1e30


LOG2E = 1.4426950408889634
CHUNK = 128

VMEM = pl.BlockSpec(memory_space=pltpu.VMEM)
SMEM = pl.BlockSpec(memory_space=pltpu.SMEM)


def nt(a, b):
    return lax.dot_general(a, b, (((1,), (1,)), ((), ())), preferred_element_type=jnp.float32)


def nn(a, b):
    return lax.dot_general(a, b, (((1,), (0,)), ((), ())), preferred_element_type=jnp.float32)


def tn(a, b):
    return lax.dot_general(a, b, (((0,), (0,)), ((), ())), preferred_element_type=jnp.float32)


def fold(a, op):
    rows = a.shape[0] // 8
    parts = a.reshape(rows, 8, a.shape[1])
    return op(parts, axis=0)


def scalars(ref, count):
    row = ref[...]
    lane = lax.broadcasted_iota(jnp.int32, row.shape, 1)
    return [jnp.sum(jnp.where(lane == i, row, 0)) for i in range(count)]


def up_down(z, flip):
    return z + 1 - 2 * ((z + flip) % 2)


def row_pairs(rows):
    pairs = ([], [])
    for z in range(rows):
        for x in range(2):
            for h in range(2):
                for way in range(2):
                    to = z + 1 - 2 * ((z + (h ^ way)) % 2)
                    other = (to, x) if 0 <= to < rows else (z, 1 - x)
                    node = 4 * z + 2 * x + h
                    pairs[way].append((node, 4 * other[0] + 2 * other[1] + h))
    return pairs


def pack_kernel(plan_ref, k_ref, v_ref, q_ref, g_ref, plan_out, kv_ref, half_ref, qg_ref, sems):
    side = lax.axis_index("head")
    dim = k_ref.shape[1]
    width = q_ref.shape[1]
    moves = (
        (k_ref, kv_ref.at[:, :dim]),
        (v_ref, kv_ref.at[:, dim:]),
        (q_ref, qg_ref.at[:, :width]),
        (g_ref, qg_ref.at[:, width:]),
        (plan_ref, plan_out),
    )
    copies = [pltpu.make_async_copy(a, b, sems.at[i]) for i, (a, b) in enumerate(moves)]
    for copy in copies:
        copy.start()
    for copy in copies[:2]:
        copy.wait()

    @pl.when(side == 0)
    def _():
        half_ref[...] = kv_ref[:, :dim]

    @pl.when(side == 1)
    def _():
        half_ref[...] = kv_ref[:, dim:]

    for copy in copies[2:]:
        copy.wait()


def loop(count, body, carry):
    if count <= 8:
        for j in range(count):
            carry = body(j, carry)
        return carry
    return lax.fori_loop(0, count, body, carry)

def rows_at(c):
    start = c * CHUNK
    return pl.ds(start if isinstance(start, int) else pl.multiple_of(start, CHUNK), CHUNK)


def contract(sizes, low, buf, ref, i):
    rounds, reach, tok, heads, head_dim = sizes
    lanes = heads * CHUNK
    span = 2 * reach + 2
    slot = slice(i * lanes, (i + 1) * lanes)
    if span <= 8:
        rows = (2 * reach + 1) * CHUNK
        at = pl.ds(pl.multiple_of((low + i) * CHUNK, CHUNK), rows)
        return tn(buf[at, :], ref[i * CHUNK:i * CHUNK + rows, slot])

    def add(j, acc):
        return acc + tn(buf[rows_at(low + j), :], ref[rows_at(j), slot])

    return lax.fori_loop(0, span, add, jnp.zeros((head_dim, lanes), jnp.float32))


def two_stretches(sizes, begin_ref, z, column, kbuf, vbuf, q_all, g_all, w_ref, p_ref, d_ref,
                  od_ref, blocks, put):
    rounds, reach, tok, heads, head_dim = sizes
    inv_root = 1.0 / math.sqrt(head_dim)
    width = heads * head_dim
    lanes = heads * CHUNK
    span = 2 * reach + 2
    unrolled = span <= 8
    low = 4 * rounds + 2 * column - 2 * reach
    low_place = (2 * (z - rounds) * tok) + low * CHUNK
    q, g, places, begin = [], [], [], []
    for i in range(2):
        rows = slice(i * CHUNK, (i + 1) * CHUNK)
        q.append(jnp.concatenate(
            [q_all[rows, h * head_dim:(h + 1) * head_dim] for h in range(heads)], axis=0))
        g.append(jnp.concatenate(
            [g_all[rows, h * head_dim:(h + 1) * head_dim] for h in range(heads)], axis=0))
        lane = lax.broadcasted_iota(jnp.int32, (1, lanes), 1) % CHUNK
        place = (2 * z + column) * tok + i * CHUNK + lane
        places.append(place)
        begin.append(begin_ref[i:i + 1, :])

    def slots(j):
        if not unrolled:
            return (0, 1)
        return tuple(i for i in range(2) if i <= j <= 2 * reach + i)

    def scores(j, tops):
        tops = list(tops)
        k = kbuf[rows_at(low + j), :]
        at = low_place + j * CHUNK + lax.broadcasted_iota(jnp.int32, (CHUNK, lanes), 0)
        for i in slots(j):
            allowed = at >= begin[i]
            if not unrolled or j == 2 * reach + i:
                allowed = allowed & (at <= places[i])
            s = jnp.where(allowed, nt(k, q[i]) * (inv_root * LOG2E), NEG)
            w_ref[i, j] = s
            tops[i] = jnp.maximum(tops[i], fold(s, jnp.max))
        return tuple(tops)

    full = lambda value: tuple(jnp.full((8, lanes), value, jnp.float32) for _ in range(2))
    tops = loop(span, scores, full(NEG))
    tops = [jnp.max(t, axis=0, keepdims=True) for t in tops]

    def exps(j, totals):
        totals = list(totals)
        for i in slots(j):
            e = jnp.exp2(w_ref[i, j] - tops[i])
            w_ref[i, j] = e
            p_ref[rows_at(j), slice(i * lanes, (i + 1) * lanes)] = e.astype(jnp.bfloat16)
            totals[i] = totals[i] + fold(e, jnp.sum)
        return tuple(totals)

    totals = loop(span, exps, full(0.0))
    scale = [1.0 / jnp.sum(t, axis=0, keepdims=True) for t in totals]
    dots = []
    for i in range(2):
        total = contract(sizes, low, vbuf, p_ref, i) * scale[i]
        attended = total.T.astype(jnp.bfloat16)
        for h in range(heads):
            od_ref[i * CHUNK:(i + 1) * CHUNK, h * head_dim:(h + 1) * head_dim] = (
                attended[h * CHUNK:(h + 1) * CHUNK])
        rounded = total.astype(jnp.bfloat16).astype(jnp.float32)
        dots.append(jnp.sum(g[i].astype(jnp.float32).T * rounded, axis=0, keepdims=True))

    def backward(j, carry):
        v = vbuf[rows_at(low + j), :]
        for i in range(2):
            if i in slots(j):
                w = w_ref[i, j] * scale[i]
                ds = (w * (nt(v, g[i]) - dots[i])).astype(jnp.bfloat16)
                d_ref[rows_at(j), slice(i * lanes, (i + 1) * lanes)] = ds
                p_ref[rows_at(j), slice(i * lanes, (i + 1) * lanes)] = w.astype(jnp.bfloat16)
            else:
                blank = jnp.zeros((CHUNK, lanes), jnp.bfloat16)
                d_ref[rows_at(j), slice(i * lanes, (i + 1) * lanes)] = blank
                p_ref[rows_at(j), slice(i * lanes, (i + 1) * lanes)] = blank
        return carry

    loop(span, backward, 0)
    q_both = jnp.concatenate(q, axis=0)
    g_both = jnp.concatenate(g, axis=0)

    def keys(m, carry):
        first, count = blocks
        b = first + 2 * m
        start = b * tok
        at = pl.ds(start if isinstance(start, int) else pl.multiple_of(start, tok), tok)
        put(count - 1 - m, nn(d_ref[at, :], q_both) * inv_root, nn(p_ref[at, :], g_both))
        return carry

    loop(blocks[1], keys, 0)


def query_grads(sizes, column, kbuf, d_ref, od_ref):
    rounds, reach, tok, heads, head_dim = sizes
    inv_root = 1.0 / math.sqrt(head_dim)
    low = 4 * rounds + 2 * column - 2 * reach
    width = heads * head_dim
    for i in range(2):
        grad = (contract(sizes, low, kbuf, d_ref, i) * inv_root).T.astype(jnp.bfloat16)
        for h in range(heads):
            at = width + h * head_dim
            od_ref[i * CHUNK:(i + 1) * CHUNK, at:at + head_dim] = (
                grad[h * CHUNK:(h + 1) * CHUNK])


def own_kernel(sizes):
    rounds, reach, tok, heads, head_dim = sizes

    def kernel(begin_ref, k_ref, v_ref, q_ref, g_ref, mine_ref, other_ref, half_ref, cross_ref,
               att_ref, d_ref, kv_out, kbuf, vbuf, w_ref, p_ref):
        here = lax.axis_index("ctx")
        side = lax.axis_index("head")
        z = here // 2
        x = here % 2

        for r in range(rounds):
            for ref, column in ((mine_ref, (x + side) % 2), (other_ref, (x + 1 - side) % 2)):
                at = pl.ds(pl.multiple_of((2 * (rounds - 1 - r) + column) * tok, tok), tok)
                kbuf[at, :] = ref[r, :, :head_dim]
                vbuf[at, :] = ref[r, :, head_dim:]
        own = pl.ds(pl.multiple_of((2 * rounds + x) * tok, tok), tok)
        kbuf[own, :] = k_ref[...]
        vbuf[own, :] = v_ref[...]
        next_to = pl.ds(pl.multiple_of((2 * rounds + 1 - x) * tok, tok), tok)

        @pl.when(side == 0)
        def _():
            kbuf[next_to, :] = half_ref[...]
            vbuf[next_to, :] = cross_ref[...]

        @pl.when(side == 1)
        def _():
            vbuf[next_to, :] = half_ref[...]
            kbuf[next_to, :] = cross_ref[...]

        def put(r, dk, dv):
            kv_out[r, :, :head_dim] = dk
            kv_out[r, :, head_dim:] = dv

        two_stretches(sizes, begin_ref, z, x, kbuf, vbuf, q_ref, g_ref, w_ref, p_ref, d_ref,
                      att_ref, (0, rounds + 1), put)

    return kernel


def next_kernel(sizes):
    rounds, reach, tok, heads, head_dim = sizes
    width = heads * head_dim

    def kernel(begin_ref, kbuf, vbuf, qg_ref, own_kv, att_ref, d_ref, kv_out, far_out,
               w_ref, p_ref, sums):
        here = lax.axis_index("ctx")
        z = here // 2
        x = here % 2
        sums[...] = own_kv[...]

        def put(r, dk, dv):
            at = r + x
            sums[at, :, :head_dim] = sums[at, :, :head_dim] + dk
            sums[at, :, head_dim:] = sums[at, :, head_dim:] + dv

        two_stretches(sizes, begin_ref, z, 1 - x, kbuf, vbuf, qg_ref.at[:, :width],
                      qg_ref.at[:, width:], w_ref, p_ref, d_ref, att_ref, (1, rounds), put)
        kv_out[...] = sums[0]
        far_out[...] = sums[1:].astype(far_out.dtype)

    return kernel


def send_kernel(sizes):
    rounds, reach, tok, heads, head_dim = sizes
    width = heads * head_dim

    def kernel(plan_ref, kbuf, d_own, d_next, att_own, att_next, od_ref, send_a, send_b):
        here = lax.axis_index("ctx")
        side = lax.axis_index("head")
        x = here % 2
        plan = scalars(plan_ref, 4)
        for at, column, att, d_ref in ((0, x, att_own, d_own), (tok, 1 - x, att_next, d_next)):
            rows = od_ref.at[at:at + tok, :]
            rows[:, :width] = att[...]
            query_grads(sizes, column, kbuf, d_ref, rows)
        for way, out in enumerate((send_a, send_b)):
            flip = (side + way) % 2
            for i in range(2):
                wanted = jnp.where(flip == 0, plan[i], plan[2 + i])
                out[i * CHUNK:(i + 1) * CHUNK, :] = od_ref[row_of(wanted, x), :]

    return kernel


def row_of(wanted, x):
    inner = wanted % 4
    return pl.ds(pl.multiple_of(((inner + 2 * x) % 4) * CHUNK, CHUNK), CHUNK)


def place_kernel(width):
    def kernel(plan_ref, row_ref, a_ref, b_ref, s_ref, t_ref, out_ref, dq_ref, dk_ref, dv_ref,
               rows_buf, dq_buf, dk_buf, dv_buf, sems):
        here = lax.axis_index("ctx")
        side = lax.axis_index("head")
        z = here // 2
        source_a = up_down(z, side)
        plan = scalars(plan_ref, 2)
        half = dk_buf.shape[1]
        copies = []

        def send(buf, out, number):
            copy = pltpu.make_async_copy(buf, out, sems.at[number])
            copy.start()
            copies.append(copy)

        dk_buf[...] = s_ref[:, :half] + t_ref[:, :half]
        send(dk_buf, dk_ref, 0)
        dv_buf[...] = s_ref[:, half:] + t_ref[:, half:]
        send(dv_buf, dv_ref, 1)
        for slot in range(2):
            wanted = plan[slot]
            to = pl.ds(slot * CHUNK, CHUNK)
            inside = row_of(wanted, here % 2)

            def put(rows):
                rows_buf[to, :] = rows[:, :width]
                dq_buf[to, :] = rows[:, width:].astype(jnp.float32)

            home = wanted // 4 == z
            from_a = wanted // 4 == source_a
            pl.when(home)(lambda: put(row_ref[inside, :]))
            pl.when(from_a)(lambda: put(a_ref[to, :]))
            pl.when(jnp.logical_not(home | from_a))(lambda: put(b_ref[to, :]))
            send(rows_buf.at[to, :], out_ref.at[to, :], 2 + 2 * slot)
            send(dq_buf.at[to, :], dq_ref.at[to, :], 3 + 2 * slot)
        for copy in copies:
            copy.wait()

    return kernel


def per_device(queries, key_input, value_input, grad_out, doc_lengths, stretch_plan):
    tok, head_dim = key_input.shape
    width = queries.shape[1]
    heads = width // head_dim
    n = lax.axis_size("ctx")
    rounds = (min(DOC_CAP, tok * n // 4) // tok + 1) // 2
    reach = 2 * rounds
    bf16, f32 = jnp.bfloat16, jnp.float32
    both = ("ctx", "head")
    cross = [(0, 1), (1, 0)]
    side = lax.axis_index("head")

    here = lax.axis_index("ctx")
    order = jnp.arange(doc_lengths.shape[0], dtype=jnp.int32)
    bounds = jnp.sum(jnp.where(order[None, :] <= order[:, None], doc_lengths[None, :], 0), axis=1)

    def begins(device):
        places = device * tok + jnp.arange(tok, dtype=jnp.int32)
        starts = jnp.max(jnp.where(bounds[:, None] <= places[None, :], bounds[:, None], 0), axis=0)
        starts = starts.reshape(tok // CHUNK, 1, CHUNK)
        return jnp.broadcast_to(starts, (tok // CHUNK, heads, CHUNK)).reshape(tok // CHUNK, -1)

    def lanes_of(values):
        return jnp.pad(values, (0, 128 - values.shape[0])).reshape(1, 128)

    def fetch_pairs(r):
        pairs = []
        for s in range(n):
            for h in range(2):
                to = s // 2 + r + 1
                column = (s + h) % 2 if to < n // 2 else s % 2
                pairs.append((2 * s + h, 2 * (2 * (to % (n // 2)) + column) + h))
        return pairs

    def back_pairs(r):
        return [(s, s - 2 * r) for s in range(2 * r, n)]

    plan_out, own_kv, half, queries_grads = pl.pallas_call(
        pack_kernel,
        out_shape=(
            pltpu.VMEM(stretch_plan.shape, jnp.int32),
            pltpu.VMEM((tok, 2 * head_dim), bf16),
            pltpu.VMEM((tok, head_dim), bf16),
            pltpu.VMEM((tok, 2 * width), bf16),
        ),
        in_specs=[pl.BlockSpec(memory_space=pl.ANY)] * 5,
        out_specs=(VMEM,) * 4,
        scratch_shapes=[pltpu.SemaphoreType.DMA((5,))],
        name="pack",
    )(stretch_plan, key_input, value_input, queries, grad_out)
    tie_a, tie_b = row_pairs(n // 2)
    near = [(i, i ^ 1) for i in range(n)]
    part = lax.ppermute(queries_grads, "ctx", near)
    half_next = lax.ppermute(half, "ctx", near)
    mine = [lax.ppermute(own_kv, both, fetch_pairs(r)) for r in range(rounds)]
    mine = jnp.stack(mine)
    other = lax.ppermute(mine, "head", cross)
    half_cross = lax.ppermute(half_next, "head", cross)
    sizes = (rounds, reach, tok, heads, head_dim)
    params = pltpu.CompilerParams(vmem_limit_bytes=40 << 20)
    span = 2 * reach + 2
    weights = pltpu.VMEM((span * CHUNK, 2 * heads * CHUNK), bf16)
    scores = pltpu.VMEM((2, span, CHUNK, heads * CHUNK), f32)
    buffer = jax.ShapeDtypeStruct(((2 * rounds + 2) * tok, head_dim), bf16)
    rows = jax.ShapeDtypeStruct((tok, 2 * width), bf16)
    attended = jax.ShapeDtypeStruct((tok, width), bf16)
    grads = jax.ShapeDtypeStruct((span * CHUNK, 2 * heads * CHUNK), bf16)
    key_sums = jax.ShapeDtypeStruct((rounds + 1, tok, 2 * head_dim), f32)
    att_own, d_own, kv_own, kbuf, vbuf = pl.pallas_call(
        own_kernel(sizes),
        out_shape=(attended, grads, key_sums, buffer, buffer),
        in_specs=[VMEM] * 9,
        out_specs=(VMEM,) * 5,
        scratch_shapes=[scores, weights],
        compiler_params=params,
        name="attend_own",
    )(begins(here), key_input, value_input, queries, grad_out, mine, other, half_next,
      half_cross)
    kv_own, stretch_here = lax.optimization_barrier((kv_own, plan_out))
    plan_mine = lax.ppermute(stretch_here, both, tie_a)
    plan_other = lax.ppermute(plan_mine, "head", cross)
    plans = jnp.where(side == 0, jnp.concatenate([plan_mine, plan_other]),
                      jnp.concatenate([plan_other, plan_mine]))
    att_next, d_next, kv_sum, far = pl.pallas_call(
        next_kernel(sizes),
        out_shape=(
            attended, grads, jax.ShapeDtypeStruct((tok, 2 * head_dim), f32),
            jax.ShapeDtypeStruct((rounds, tok, 2 * head_dim), bf16),
        ),
        in_specs=[VMEM] * 5,
        out_specs=(VMEM,) * 4,
        scratch_shapes=[scores, weights, pltpu.VMEM((rounds + 1, tok, 2 * head_dim), f32)],
        compiler_params=params,
        name="attend_next",
    )(begins(here ^ 1), kbuf, vbuf, part, kv_own)
    od, send_a, send_b = pl.pallas_call(
        send_kernel(sizes),
        out_shape=(jax.ShapeDtypeStruct((2 * tok, 2 * width), bf16), rows, rows),
        in_specs=[VMEM] * 6,
        out_specs=(VMEM,) * 3,
        compiler_params=params,
        name="send_rows",
    )(lanes_of(plans), kbuf, d_own, d_next, att_own, att_next)

    moved_a = lax.ppermute(send_a, both, tie_a)
    moved_b = lax.ppermute(send_b, both, tie_b)
    total = kv_sum
    for r in range(rounds):
        total = total + lax.ppermute(far[r], "ctx", back_pairs(r + 1)).astype(f32)
    total_other = lax.ppermute(total, "head", cross)

    output, query_grad, key_grad, value_grad = pl.pallas_call(
        place_kernel(width),
        out_shape=(
            jax.ShapeDtypeStruct((tok, width), bf16),
            jax.ShapeDtypeStruct((tok, width), f32),
            jax.ShapeDtypeStruct((tok, head_dim), f32),
            jax.ShapeDtypeStruct((tok, head_dim), f32),
        ),
        in_specs=[VMEM] * 6,
        out_specs=(pl.BlockSpec(memory_space=pl.ANY),) * 4,
        scratch_shapes=[
            pltpu.VMEM((tok, width), bf16), pltpu.VMEM((tok, width), f32),
            pltpu.VMEM((tok, head_dim), f32), pltpu.VMEM((tok, head_dim), f32),
            pltpu.SemaphoreType.DMA((6,)),
        ],
        compiler_params=pltpu.CompilerParams(vmem_limit_bytes=32 << 20),
        name="place",
    )(lanes_of(stretch_plan), od, moved_a, moved_b, total, total_other)
    return (output, query_grad, key_grad, value_grad)


def solution(mesh):
    return jax.shard_map(
        per_device,
        mesh=mesh,
        in_specs=(
            P(("groups", "ctx"), "head"),
            P(("groups", "ctx"), None),
            P(("groups", "ctx"), None),
            P(("groups", "ctx"), "head"),
            P("groups"),
            P(("groups", "ctx")),
        ),
        out_specs=(
            P(("groups", "ctx"), "head"),
            P(("groups", "ctx"), "head"),
            P(("groups", "ctx"), None),
            P(("groups", "ctx"), None),
        ),
        check_vma=False,
    )
```

```python
import math

import jax
import jax.numpy as jnp
from jax import lax
from jax.experimental import pallas as pl
from jax.experimental.pallas import tpu as pltpu
from jax.sharding import PartitionSpec as P

DOC_CAP = 4096
NEG = -1e30


LOG2E = 1.4426950408889634
CHUNK = 128

VMEM = pl.BlockSpec(memory_space=pltpu.VMEM)
SMEM = pl.BlockSpec(memory_space=pltpu.SMEM)


def nt(a, b):
    return lax.dot_general(a, b, (((1,), (1,)), ((), ())), preferred_element_type=jnp.float32)


def nn(a, b):
    return lax.dot_general(a, b, (((1,), (0,)), ((), ())), preferred_element_type=jnp.float32)


def tn(a, b):
    return lax.dot_general(a, b, (((0,), (0,)), ((), ())), preferred_element_type=jnp.float32)


def fold(a, op):
    rows = a.shape[0] // 8
    parts = a.reshape(rows, 8, a.shape[1])
    return op(parts, axis=0)


def scalars(ref, count):
    row = ref[...]
    lane = lax.broadcasted_iota(jnp.int32, row.shape, 1)
    return [jnp.sum(jnp.where(lane == i, row, 0)) for i in range(count)]


def up_down(z, flip):
    return z + 1 - 2 * ((z + flip) % 2)


def row_pairs(rows):
    pairs = ([], [])
    for z in range(rows):
        for x in range(2):
            for h in range(2):
                for way in range(2):
                    to = z + 1 - 2 * ((z + (h ^ way)) % 2)
                    other = (to, x) if 0 <= to < rows else (z, 1 - x)
                    node = 4 * z + 2 * x + h
                    pairs[way].append((node, 4 * other[0] + 2 * other[1] + h))
    return pairs


def pack_kernel(plan_ref, k_ref, v_ref, q_ref, g_ref, plan_out, kv_ref, half_ref, qg_ref, sems):
    side = lax.axis_index("head")
    dim = k_ref.shape[1]
    width = q_ref.shape[1]
    moves = (
        (k_ref, kv_ref.at[:, :dim]),
        (v_ref, kv_ref.at[:, dim:]),
        (q_ref, qg_ref.at[:, :width]),
        (g_ref, qg_ref.at[:, width:]),
        (plan_ref, plan_out),
    )
    copies = [pltpu.make_async_copy(a, b, sems.at[i]) for i, (a, b) in enumerate(moves)]
    for copy in copies:
        copy.start()
    for copy in copies[:2]:
        copy.wait()

    @pl.when(side == 0)
    def _():
        half_ref[...] = kv_ref[:, :dim]

    @pl.when(side == 1)
    def _():
        half_ref[...] = kv_ref[:, dim:]

    for copy in copies[2:]:
        copy.wait()


def loop(count, body, carry):
    if count <= 8:
        for j in range(count):
            carry = body(j, carry)
        return carry
    return lax.fori_loop(0, count, body, carry)

def rows_at(c):
    start = c * CHUNK
    return pl.ds(start if isinstance(start, int) else pl.multiple_of(start, CHUNK), CHUNK)


def contract(sizes, low, buf, ref, i):
    rounds, reach, tok, heads, head_dim = sizes
    lanes = heads * CHUNK
    span = 2 * reach + 2
    slot = slice(i * lanes, (i + 1) * lanes)
    if span <= 8:
        rows = (2 * reach + 1) * CHUNK
        at = pl.ds(pl.multiple_of((low + i) * CHUNK, CHUNK), rows)
        return tn(buf[at, :], ref[i * CHUNK:i * CHUNK + rows, slot])

    def add(j, acc):
        return acc + tn(buf[rows_at(low + j), :], ref[rows_at(j), slot])

    return lax.fori_loop(0, span, add, jnp.zeros((head_dim, lanes), jnp.float32))


def two_stretches(sizes, begin_ref, z, column, kbuf, vbuf, q_all, g_all, w_ref, p_ref, d_ref,
                  od_ref, blocks, put):
    rounds, reach, tok, heads, head_dim = sizes
    inv_root = 1.0 / math.sqrt(head_dim)
    width = heads * head_dim
    lanes = heads * CHUNK
    span = 2 * reach + 2
    unrolled = span <= 8
    low = 4 * rounds + 2 * column - 2 * reach
    low_place = (2 * (z - rounds) * tok) + low * CHUNK
    q, g, places, begin = [], [], [], []
    for i in range(2):
        rows = slice(i * CHUNK, (i + 1) * CHUNK)
        q.append(jnp.concatenate(
            [q_all[rows, h * head_dim:(h + 1) * head_dim] for h in range(heads)], axis=0))
        g.append(jnp.concatenate(
            [g_all[rows, h * head_dim:(h + 1) * head_dim] for h in range(heads)], axis=0))
        lane = lax.broadcasted_iota(jnp.int32, (1, lanes), 1) % CHUNK
        place = (2 * z + column) * tok + i * CHUNK + lane
        places.append(place)
        begin.append(begin_ref[i:i + 1, :])

    def slots(j):
        if not unrolled:
            return (0, 1)
        return tuple(i for i in range(2) if i <= j <= 2 * reach + i)

    def scores(j, tops):
        tops = list(tops)
        k = kbuf[rows_at(low + j), :]
        at = low_place + j * CHUNK + lax.broadcasted_iota(jnp.int32, (CHUNK, lanes), 0)
        for i in slots(j):
            allowed = at >= begin[i]
            if not unrolled or j == 2 * reach + i:
                allowed = allowed & (at <= places[i])
            s = jnp.where(allowed, nt(k, q[i]) * (inv_root * LOG2E), NEG)
            w_ref[i, j] = s
            tops[i] = jnp.maximum(tops[i], fold(s, jnp.max))
        return tuple(tops)

    full = lambda value: tuple(jnp.full((8, lanes), value, jnp.float32) for _ in range(2))
    tops = loop(span, scores, full(NEG))
    tops = [jnp.max(t, axis=0, keepdims=True) for t in tops]

    def exps(j, totals):
        totals = list(totals)
        for i in slots(j):
            e = jnp.exp2(w_ref[i, j] - tops[i])
            w_ref[i, j] = e
            p_ref[rows_at(j), slice(i * lanes, (i + 1) * lanes)] = e.astype(jnp.bfloat16)
            totals[i] = totals[i] + fold(e, jnp.sum)
        return tuple(totals)

    totals = loop(span, exps, full(0.0))
    scale = [1.0 / jnp.sum(t, axis=0, keepdims=True) for t in totals]
    dots = []
    for i in range(2):
        total = contract(sizes, low, vbuf, p_ref, i) * scale[i]
        attended = total.T.astype(jnp.bfloat16)
        for h in range(heads):
            od_ref[i * CHUNK:(i + 1) * CHUNK, h * head_dim:(h + 1) * head_dim] = (
                attended[h * CHUNK:(h + 1) * CHUNK])
        rounded = total.astype(jnp.bfloat16).astype(jnp.float32)
        dots.append(jnp.sum(g[i].astype(jnp.float32).T * rounded, axis=0, keepdims=True))

    def backward(j, carry):
        v = vbuf[rows_at(low + j), :]
        for i in range(2):
            if i in slots(j):
                w = w_ref[i, j] * scale[i]
                ds = (w * (nt(v, g[i]) - dots[i])).astype(jnp.bfloat16)
                d_ref[rows_at(j), slice(i * lanes, (i + 1) * lanes)] = ds
                p_ref[rows_at(j), slice(i * lanes, (i + 1) * lanes)] = w.astype(jnp.bfloat16)
            else:
                blank = jnp.zeros((CHUNK, lanes), jnp.bfloat16)
                d_ref[rows_at(j), slice(i * lanes, (i + 1) * lanes)] = blank
                p_ref[rows_at(j), slice(i * lanes, (i + 1) * lanes)] = blank
        return carry

    loop(span, backward, 0)
    q_both = jnp.concatenate(q, axis=0)
    g_both = jnp.concatenate(g, axis=0)

    def keys(m, carry):
        first, count = blocks
        b = first + 2 * m
        start = b * tok
        at = pl.ds(start if isinstance(start, int) else pl.multiple_of(start, tok), tok)
        put(count - 1 - m, nn(d_ref[at, :], q_both) * inv_root, nn(p_ref[at, :], g_both))
        return carry

    loop(blocks[1], keys, 0)


def query_grads(sizes, column, kbuf, d_ref, od_ref):
    rounds, reach, tok, heads, head_dim = sizes
    inv_root = 1.0 / math.sqrt(head_dim)
    low = 4 * rounds + 2 * column - 2 * reach
    width = heads * head_dim
    for i in range(2):
        grad = (contract(sizes, low, kbuf, d_ref, i) * inv_root).T.astype(jnp.bfloat16)
        for h in range(heads):
            at = width + h * head_dim
            od_ref[i * CHUNK:(i + 1) * CHUNK, at:at + head_dim] = (
                grad[h * CHUNK:(h + 1) * CHUNK])


def own_kernel(sizes):
    rounds, reach, tok, heads, head_dim = sizes

    def kernel(begin_ref, k_ref, v_ref, q_ref, g_ref, mine_ref, other_ref, half_ref, cross_ref,
               att_ref, d_ref, kv_out, kbuf, vbuf, w_ref, p_ref):
        here = lax.axis_index("ctx")
        side = lax.axis_index("head")
        z = here // 2
        x = here % 2

        for r in range(rounds):
            for ref, column in ((mine_ref, (x + side) % 2), (other_ref, (x + 1 - side) % 2)):
                at = pl.ds(pl.multiple_of((2 * (rounds - 1 - r) + column) * tok, tok), tok)
                kbuf[at, :] = ref[r, :, :head_dim]
                vbuf[at, :] = ref[r, :, head_dim:]
        own = pl.ds(pl.multiple_of((2 * rounds + x) * tok, tok), tok)
        kbuf[own, :] = k_ref[...]
        vbuf[own, :] = v_ref[...]
        next_to = pl.ds(pl.multiple_of((2 * rounds + 1 - x) * tok, tok), tok)

        @pl.when(side == 0)
        def _():
            kbuf[next_to, :] = half_ref[...]
            vbuf[next_to, :] = cross_ref[...]

        @pl.when(side == 1)
        def _():
            vbuf[next_to, :] = half_ref[...]
            kbuf[next_to, :] = cross_ref[...]

        def put(r, dk, dv):
            kv_out[r, :, :head_dim] = dk
            kv_out[r, :, head_dim:] = dv

        two_stretches(sizes, begin_ref, z, x, kbuf, vbuf, q_ref, g_ref, w_ref, p_ref, d_ref,
                      att_ref, (0, rounds + 1), put)

    return kernel


def next_kernel(sizes):
    rounds, reach, tok, heads, head_dim = sizes
    width = heads * head_dim

    def kernel(begin_ref, kbuf, vbuf, qg_ref, own_kv, att_ref, d_ref, kv_out, far_out,
               w_ref, p_ref, sums):
        here = lax.axis_index("ctx")
        z = here // 2
        x = here % 2
        def put(r, dk, dv):
            sums[r, :, :head_dim] = dk
            sums[r, :, head_dim:] = dv

        two_stretches(sizes, begin_ref, z, 1 - x, kbuf, vbuf, qg_ref.at[:, :width],
                      qg_ref.at[:, width:], w_ref, p_ref, d_ref, att_ref, (1, rounds), put)
        here_first = x == 0
        kv_out[...] = own_kv[0] + jnp.where(here_first, sums[0], 0.0)
        for r in range(rounds):
            term = jnp.where(here_first, sums[r + 1] if r + 1 < rounds else 0.0, sums[r])
            far_out[r] = (own_kv[r + 1] + term).astype(far_out.dtype)

    return kernel


def send_kernel(sizes):
    rounds, reach, tok, heads, head_dim = sizes
    width = heads * head_dim

    def kernel(plan_ref, kbuf, d_own, d_next, att_own, att_next, od_ref, send_a, send_b):
        here = lax.axis_index("ctx")
        side = lax.axis_index("head")
        x = here % 2
        plan = scalars(plan_ref, 4)
        for at, column, att, d_ref in ((0, x, att_own, d_own), (tok, 1 - x, att_next, d_next)):
            rows = od_ref.at[at:at + tok, :]
            rows[:, :width] = att[...]
            query_grads(sizes, column, kbuf, d_ref, rows)
        for way, out in enumerate((send_a, send_b)):
            flip = (side + way) % 2
            for i in range(2):
                wanted = jnp.where(flip == 0, plan[i], plan[2 + i])
                out[i * CHUNK:(i + 1) * CHUNK, :] = od_ref[row_of(wanted, x), :]

    return kernel


def row_of(wanted, x):
    inner = wanted % 4
    return pl.ds(pl.multiple_of(((inner + 2 * x) % 4) * CHUNK, CHUNK), CHUNK)


def place_kernel(width):
    def kernel(plan_ref, row_ref, a_ref, b_ref, s_ref, t_ref, out_ref, dq_ref, dk_ref, dv_ref,
               rows_buf, dq_buf, dk_buf, dv_buf, sems):
        here = lax.axis_index("ctx")
        side = lax.axis_index("head")
        z = here // 2
        source_a = up_down(z, side)
        plan = scalars(plan_ref, 2)
        half = dk_buf.shape[1]
        copies = []

        def send(buf, out, number):
            copy = pltpu.make_async_copy(buf, out, sems.at[number])
            copy.start()
            copies.append(copy)

        dk_buf[...] = s_ref[:, :half] + t_ref[:, :half]
        send(dk_buf, dk_ref, 0)
        dv_buf[...] = s_ref[:, half:] + t_ref[:, half:]
        send(dv_buf, dv_ref, 1)
        for slot in range(2):
            wanted = plan[slot]
            to = pl.ds(slot * CHUNK, CHUNK)
            inside = row_of(wanted, here % 2)

            def put(rows):
                rows_buf[to, :] = rows[:, :width]
                dq_buf[to, :] = rows[:, width:].astype(jnp.float32)

            home = wanted // 4 == z
            from_a = wanted // 4 == source_a
            pl.when(home)(lambda: put(row_ref[inside, :]))
            pl.when(from_a)(lambda: put(a_ref[to, :]))
            pl.when(jnp.logical_not(home | from_a))(lambda: put(b_ref[to, :]))
            send(rows_buf.at[to, :], out_ref.at[to, :], 2 + 2 * slot)
            send(dq_buf.at[to, :], dq_ref.at[to, :], 3 + 2 * slot)
        for copy in copies:
            copy.wait()

    return kernel


def per_device(queries, key_input, value_input, grad_out, doc_lengths, stretch_plan):
    tok, head_dim = key_input.shape
    width = queries.shape[1]
    heads = width // head_dim
    n = lax.axis_size("ctx")
    rounds = (min(DOC_CAP, tok * n // 4) // tok + 1) // 2
    reach = 2 * rounds
    bf16, f32 = jnp.bfloat16, jnp.float32
    both = ("ctx", "head")
    cross = [(0, 1), (1, 0)]
    side = lax.axis_index("head")

    here = lax.axis_index("ctx")
    order = jnp.arange(doc_lengths.shape[0], dtype=jnp.int32)
    bounds = jnp.sum(jnp.where(order[None, :] <= order[:, None], doc_lengths[None, :], 0), axis=1)

    def begins(device):
        places = device * tok + jnp.arange(tok, dtype=jnp.int32)
        starts = jnp.max(jnp.where(bounds[:, None] <= places[None, :], bounds[:, None], 0), axis=0)
        starts = starts.reshape(tok // CHUNK, 1, CHUNK)
        return jnp.broadcast_to(starts, (tok // CHUNK, heads, CHUNK)).reshape(tok // CHUNK, -1)

    def lanes_of(values):
        return jnp.pad(values, (0, 128 - values.shape[0])).reshape(1, 128)

    def fetch_pairs(r):
        pairs = []
        for s in range(n):
            for h in range(2):
                to = s // 2 + r + 1
                column = (s + h) % 2 if to < n // 2 else s % 2
                pairs.append((2 * s + h, 2 * (2 * (to % (n // 2)) + column) + h))
        return pairs

    def back_pairs(r):
        return [(s, s - 2 * r) for s in range(2 * r, n)]

    plan_out, own_kv, half, queries_grads = pl.pallas_call(
        pack_kernel,
        out_shape=(
            pltpu.VMEM(stretch_plan.shape, jnp.int32),
            pltpu.VMEM((tok, 2 * head_dim), bf16),
            pltpu.VMEM((tok, head_dim), bf16),
            pltpu.VMEM((tok, 2 * width), bf16),
        ),
        in_specs=[pl.BlockSpec(memory_space=pl.ANY)] * 5,
        out_specs=(VMEM,) * 4,
        scratch_shapes=[pltpu.SemaphoreType.DMA((5,))],
        name="pack",
    )(stretch_plan, key_input, value_input, queries, grad_out)
    tie_a, tie_b = row_pairs(n // 2)
    near = [(i, i ^ 1) for i in range(n)]
    part = lax.ppermute(queries_grads, "ctx", near)
    half_next = lax.ppermute(half, "ctx", near)
    mine = [lax.ppermute(own_kv, both, fetch_pairs(r)) for r in range(rounds)]
    mine = jnp.stack(mine)
    other = lax.ppermute(mine, "head", cross)
    half_cross = lax.ppermute(half_next, "head", cross)
    sizes = (rounds, reach, tok, heads, head_dim)
    params = pltpu.CompilerParams(vmem_limit_bytes=40 << 20)
    span = 2 * reach + 2
    weights = pltpu.VMEM((span * CHUNK, 2 * heads * CHUNK), bf16)
    scores = pltpu.VMEM((2, span, CHUNK, heads * CHUNK), f32)
    buffer = jax.ShapeDtypeStruct(((2 * rounds + 2) * tok, head_dim), bf16)
    rows = jax.ShapeDtypeStruct((tok, 2 * width), bf16)
    attended = jax.ShapeDtypeStruct((tok, width), bf16)
    grads = jax.ShapeDtypeStruct((span * CHUNK, 2 * heads * CHUNK), bf16)
    key_sums = jax.ShapeDtypeStruct((rounds + 1, tok, 2 * head_dim), f32)
    att_own, d_own, kv_own, kbuf, vbuf = pl.pallas_call(
        own_kernel(sizes),
        out_shape=(attended, grads, key_sums, buffer, buffer),
        in_specs=[VMEM] * 9,
        out_specs=(VMEM,) * 5,
        scratch_shapes=[scores, weights],
        compiler_params=params,
        name="attend_own",
    )(begins(here), key_input, value_input, queries, grad_out, mine, other, half_next,
      half_cross)
    kv_own, stretch_here = lax.optimization_barrier((kv_own, plan_out))
    plan_mine = lax.ppermute(stretch_here, both, tie_a)
    plan_other = lax.ppermute(plan_mine, "head", cross)
    plans = jnp.where(side == 0, jnp.concatenate([plan_mine, plan_other]),
                      jnp.concatenate([plan_other, plan_mine]))
    att_next, d_next, kv_sum, far = pl.pallas_call(
        next_kernel(sizes),
        out_shape=(
            attended, grads, jax.ShapeDtypeStruct((tok, 2 * head_dim), f32),
            jax.ShapeDtypeStruct((rounds, tok, 2 * head_dim), bf16),
        ),
        in_specs=[VMEM] * 5,
        out_specs=(VMEM,) * 4,
        scratch_shapes=[scores, weights, pltpu.VMEM((rounds, tok, 2 * head_dim), f32)],
        compiler_params=params,
        name="attend_next",
    )(begins(here ^ 1), kbuf, vbuf, part, kv_own)
    od, send_a, send_b = pl.pallas_call(
        send_kernel(sizes),
        out_shape=(jax.ShapeDtypeStruct((2 * tok, 2 * width), bf16), rows, rows),
        in_specs=[VMEM] * 6,
        out_specs=(VMEM,) * 3,
        compiler_params=params,
        name="send_rows",
    )(lanes_of(plans), kbuf, d_own, d_next, att_own, att_next)

    moved_a = lax.ppermute(send_a, both, tie_a)
    moved_b = lax.ppermute(send_b, both, tie_b)
    total = kv_sum
    for r in range(rounds):
        total = total + lax.ppermute(far[r], "ctx", back_pairs(r + 1)).astype(f32)
    total_other = lax.ppermute(total, "head", cross)

    output, query_grad, key_grad, value_grad = pl.pallas_call(
        place_kernel(width),
        out_shape=(
            jax.ShapeDtypeStruct((tok, width), bf16),
            jax.ShapeDtypeStruct((tok, width), f32),
            jax.ShapeDtypeStruct((tok, head_dim), f32),
            jax.ShapeDtypeStruct((tok, head_dim), f32),
        ),
        in_specs=[VMEM] * 6,
        out_specs=(pl.BlockSpec(memory_space=pl.ANY),) * 4,
        scratch_shapes=[
            pltpu.VMEM((tok, width), bf16), pltpu.VMEM((tok, width), f32),
            pltpu.VMEM((tok, head_dim), f32), pltpu.VMEM((tok, head_dim), f32),
            pltpu.SemaphoreType.DMA((6,)),
        ],
        compiler_params=pltpu.CompilerParams(vmem_limit_bytes=32 << 20),
        name="place",
    )(lanes_of(stretch_plan), od, moved_a, moved_b, total, total_other)
    return (output, query_grad, key_grad, value_grad)


def solution(mesh):
    return jax.shard_map(
        per_device,
        mesh=mesh,
        in_specs=(
            P(("groups", "ctx"), "head"),
            P(("groups", "ctx"), None),
            P(("groups", "ctx"), None),
            P(("groups", "ctx"), "head"),
            P("groups"),
            P(("groups", "ctx")),
        ),
        out_specs=(
            P(("groups", "ctx"), "head"),
            P(("groups", "ctx"), "head"),
            P(("groups", "ctx"), None),
            P(("groups", "ctx"), None),
        ),
        check_vma=False,
    )
```

```python
import math

import jax
import jax.numpy as jnp
from jax import lax
from jax.experimental import pallas as pl
from jax.experimental.pallas import tpu as pltpu
from jax.sharding import PartitionSpec as P

DOC_CAP = 4096
NEG = -1e30


LOG2E = 1.4426950408889634
CHUNK = 128

VMEM = pl.BlockSpec(memory_space=pltpu.VMEM)
SMEM = pl.BlockSpec(memory_space=pltpu.SMEM)


def nt(a, b):
    return lax.dot_general(a, b, (((1,), (1,)), ((), ())), preferred_element_type=jnp.float32)


def nn(a, b):
    return lax.dot_general(a, b, (((1,), (0,)), ((), ())), preferred_element_type=jnp.float32)


def tn(a, b):
    return lax.dot_general(a, b, (((0,), (0,)), ((), ())), preferred_element_type=jnp.float32)


def fold(a, op):
    rows = a.shape[0] // 8
    parts = a.reshape(rows, 8, a.shape[1])
    return op(parts, axis=0)


def scalars(ref, count):
    row = ref[...]
    lane = lax.broadcasted_iota(jnp.int32, row.shape, 1)
    return [jnp.sum(jnp.where(lane == i, row, 0)) for i in range(count)]


def up_down(z, flip):
    return z + 1 - 2 * ((z + flip) % 2)


def row_pairs(rows):
    pairs = ([], [])
    for z in range(rows):
        for x in range(2):
            for h in range(2):
                for way in range(2):
                    to = z + 1 - 2 * ((z + (h ^ way)) % 2)
                    other = (to, x) if 0 <= to < rows else (z, 1 - x)
                    node = 4 * z + 2 * x + h
                    pairs[way].append((node, 4 * other[0] + 2 * other[1] + h))
    return pairs


def pack_kernel(plan_ref, k_ref, v_ref, q_ref, g_ref, plan_out, kv_ref, half_ref, qg_ref, sems):
    side = lax.axis_index("head")
    dim = k_ref.shape[1]
    width = q_ref.shape[1]
    moves = (
        (k_ref, kv_ref.at[:, :dim]),
        (v_ref, kv_ref.at[:, dim:]),
        (q_ref, qg_ref.at[:, :width]),
        (g_ref, qg_ref.at[:, width:]),
        (plan_ref, plan_out),
    )
    copies = [pltpu.make_async_copy(a, b, sems.at[i]) for i, (a, b) in enumerate(moves)]
    for copy in copies:
        copy.start()
    for copy in copies[:2]:
        copy.wait()

    @pl.when(side == 0)
    def _():
        half_ref[...] = kv_ref[:, :dim]

    @pl.when(side == 1)
    def _():
        half_ref[...] = kv_ref[:, dim:]

    for copy in copies[2:]:
        copy.wait()


def loop(count, body, carry):
    if count <= 8:
        for j in range(count):
            carry = body(j, carry)
        return carry
    return lax.fori_loop(0, count, body, carry)

def rows_at(c):
    start = c * CHUNK
    return pl.ds(start if isinstance(start, int) else pl.multiple_of(start, CHUNK), CHUNK)


def contract(sizes, low, buf, ref, i):
    rounds, reach, tok, heads, head_dim = sizes
    lanes = heads * CHUNK
    span = 2 * reach + 2
    slot = slice(i * lanes, (i + 1) * lanes)
    if span <= 8:
        rows = (2 * reach + 1) * CHUNK
        at = pl.ds(pl.multiple_of((low + i) * CHUNK, CHUNK), rows)
        return tn(buf[at, :], ref[i * CHUNK:i * CHUNK + rows, slot])

    def add(j, acc):
        return acc + tn(buf[rows_at(low + j), :], ref[rows_at(j), slot])

    return lax.fori_loop(0, span, add, jnp.zeros((head_dim, lanes), jnp.float32))


def two_stretches(sizes, begin_ref, z, column, kbuf, vbuf, q_all, g_all, w_ref, p_ref, d_ref,
                  od_ref, blocks, put):
    rounds, reach, tok, heads, head_dim = sizes
    inv_root = 1.0 / math.sqrt(head_dim)
    width = heads * head_dim
    lanes = heads * CHUNK
    span = 2 * reach + 2
    unrolled = span <= 8
    low = 4 * rounds + 2 * column - 2 * reach
    low_place = (2 * (z - rounds) * tok) + low * CHUNK
    q, g, places, begin = [], [], [], []
    for i in range(2):
        rows = slice(i * CHUNK, (i + 1) * CHUNK)
        q.append(jnp.concatenate(
            [q_all[rows, h * head_dim:(h + 1) * head_dim] for h in range(heads)], axis=0))
        g.append(jnp.concatenate(
            [g_all[rows, h * head_dim:(h + 1) * head_dim] for h in range(heads)], axis=0))
        lane = lax.broadcasted_iota(jnp.int32, (1, lanes), 1) % CHUNK
        place = (2 * z + column) * tok + i * CHUNK + lane
        places.append(place)
        begin.append(begin_ref[i:i + 1, :])

    def slots(j):
        if not unrolled:
            return (0, 1)
        return tuple(i for i in range(2) if i <= j <= 2 * reach + i)

    def scores(j, tops):
        tops = list(tops)
        k = kbuf[rows_at(low + j), :]
        at = low_place + j * CHUNK + lax.broadcasted_iota(jnp.int32, (CHUNK, lanes), 0)
        for i in slots(j):
            allowed = at >= begin[i]
            if not unrolled or j == 2 * reach + i:
                allowed = allowed & (at <= places[i])
            s = jnp.where(allowed, nt(k, q[i]) * (inv_root * LOG2E), NEG)
            w_ref[i, j] = s
            tops[i] = jnp.maximum(tops[i], fold(s, jnp.max))
        return tuple(tops)

    full = lambda value: tuple(jnp.full((8, lanes), value, jnp.float32) for _ in range(2))
    tops = loop(span, scores, full(NEG))
    tops = [jnp.max(t, axis=0, keepdims=True) for t in tops]

    def exps(j, totals):
        totals = list(totals)
        for i in slots(j):
            e = jnp.exp2(w_ref[i, j] - tops[i])
            w_ref[i, j] = e
            p_ref[rows_at(j), slice(i * lanes, (i + 1) * lanes)] = e.astype(jnp.bfloat16)
            totals[i] = totals[i] + fold(e, jnp.sum)
        return tuple(totals)

    totals = loop(span, exps, full(0.0))
    scale = [1.0 / jnp.sum(t, axis=0, keepdims=True) for t in totals]
    dots = []
    for i in range(2):
        total = contract(sizes, low, vbuf, p_ref, i) * scale[i]
        attended = total.astype(jnp.bfloat16)
        od_ref[i * head_dim:(i + 1) * head_dim, :] = attended
        rounded = attended.astype(jnp.float32)
        dots.append(jnp.sum(g[i].astype(jnp.float32).T * rounded, axis=0, keepdims=True))

    def backward(j, carry):
        v = vbuf[rows_at(low + j), :]
        for i in range(2):
            if i in slots(j):
                w = w_ref[i, j] * scale[i]
                ds = (w * (nt(v, g[i]) - dots[i])).astype(jnp.bfloat16)
                d_ref[rows_at(j), slice(i * lanes, (i + 1) * lanes)] = ds
                p_ref[rows_at(j), slice(i * lanes, (i + 1) * lanes)] = w.astype(jnp.bfloat16)
            else:
                blank = jnp.zeros((CHUNK, lanes), jnp.bfloat16)
                d_ref[rows_at(j), slice(i * lanes, (i + 1) * lanes)] = blank
                p_ref[rows_at(j), slice(i * lanes, (i + 1) * lanes)] = blank
        return carry

    loop(span, backward, 0)
    q_both = jnp.concatenate(q, axis=0)
    g_both = jnp.concatenate(g, axis=0)

    def keys(m, carry):
        first, count = blocks
        b = first + 2 * m
        start = b * tok
        at = pl.ds(start if isinstance(start, int) else pl.multiple_of(start, tok), tok)
        put(count - 1 - m, nn(d_ref[at, :], q_both) * inv_root, nn(p_ref[at, :], g_both))
        return carry

    loop(blocks[1], keys, 0)


def query_grads(sizes, column, kbuf, d_ref, od_ref):
    rounds, reach, tok, heads, head_dim = sizes
    inv_root = 1.0 / math.sqrt(head_dim)
    low = 4 * rounds + 2 * column - 2 * reach
    width = heads * head_dim
    for i in range(2):
        grad = (contract(sizes, low, kbuf, d_ref, i) * inv_root).T.astype(jnp.bfloat16)
        for h in range(heads):
            at = width + h * head_dim
            od_ref[i * CHUNK:(i + 1) * CHUNK, at:at + head_dim] = (
                grad[h * CHUNK:(h + 1) * CHUNK])


def own_kernel(sizes):
    rounds, reach, tok, heads, head_dim = sizes

    def kernel(begin_ref, k_ref, v_ref, q_ref, g_ref, mine_ref, other_ref, half_ref, cross_ref,
               att_ref, d_ref, kv_out, kbuf, vbuf, w_ref, p_ref):
        here = lax.axis_index("ctx")
        side = lax.axis_index("head")
        z = here // 2
        x = here % 2

        for r in range(rounds):
            for ref, column in ((mine_ref, (x + side) % 2), (other_ref, (x + 1 - side) % 2)):
                at = pl.ds(pl.multiple_of((2 * (rounds - 1 - r) + column) * tok, tok), tok)
                kbuf[at, :] = ref[r, :, :head_dim]
                vbuf[at, :] = ref[r, :, head_dim:]
        own = pl.ds(pl.multiple_of((2 * rounds + x) * tok, tok), tok)
        kbuf[own, :] = k_ref[...]
        vbuf[own, :] = v_ref[...]
        next_to = pl.ds(pl.multiple_of((2 * rounds + 1 - x) * tok, tok), tok)

        @pl.when(side == 0)
        def _():
            kbuf[next_to, :] = half_ref[...]
            vbuf[next_to, :] = cross_ref[...]

        @pl.when(side == 1)
        def _():
            vbuf[next_to, :] = half_ref[...]
            kbuf[next_to, :] = cross_ref[...]

        def put(r, dk, dv):
            kv_out[r, :, :head_dim] = dk
            kv_out[r, :, head_dim:] = dv

        two_stretches(sizes, begin_ref, z, x, kbuf, vbuf, q_ref, g_ref, w_ref, p_ref, d_ref,
                      att_ref, (0, rounds + 1), put)

    return kernel


def next_kernel(sizes):
    rounds, reach, tok, heads, head_dim = sizes
    width = heads * head_dim

    def kernel(begin_ref, kbuf, vbuf, qg_ref, own_kv, att_ref, d_ref, kv_out, far_out,
               w_ref, p_ref, sums):
        here = lax.axis_index("ctx")
        z = here // 2
        x = here % 2
        def put(r, dk, dv):
            sums[r, :, :head_dim] = dk
            sums[r, :, head_dim:] = dv

        two_stretches(sizes, begin_ref, z, 1 - x, kbuf, vbuf, qg_ref.at[:, :width],
                      qg_ref.at[:, width:], w_ref, p_ref, d_ref, att_ref, (1, rounds), put)
        here_first = x == 0
        kv_out[...] = own_kv[0] + jnp.where(here_first, sums[0], 0.0)
        for r in range(rounds):
            term = jnp.where(here_first, sums[r + 1] if r + 1 < rounds else 0.0, sums[r])
            far_out[r] = (own_kv[r + 1] + term).astype(far_out.dtype)

    return kernel


def send_kernel(sizes):
    rounds, reach, tok, heads, head_dim = sizes
    width = heads * head_dim

    def kernel(plan_ref, kbuf, d_own, d_next, att_own, att_next, od_ref, send_a, send_b):
        here = lax.axis_index("ctx")
        side = lax.axis_index("head")
        x = here % 2
        plan = scalars(plan_ref, 4)
        for at, column, att, d_ref in ((0, x, att_own, d_own), (tok, 1 - x, att_next, d_next)):
            rows = od_ref.at[at:at + tok, :]
            for i in range(2):
                turned = att[i * head_dim:(i + 1) * head_dim, :].astype(jnp.float32).T
                for h in range(heads):
                    rows[i * CHUNK:(i + 1) * CHUNK, h * head_dim:(h + 1) * head_dim] = (
                        turned[h * CHUNK:(h + 1) * CHUNK].astype(jnp.bfloat16))
            query_grads(sizes, column, kbuf, d_ref, rows)
        for way, out in enumerate((send_a, send_b)):
            flip = (side + way) % 2
            for i in range(2):
                wanted = jnp.where(flip == 0, plan[i], plan[2 + i])
                out[i * CHUNK:(i + 1) * CHUNK, :] = od_ref[row_of(wanted, x), :]

    return kernel


def row_of(wanted, x):
    inner = wanted % 4
    return pl.ds(pl.multiple_of(((inner + 2 * x) % 4) * CHUNK, CHUNK), CHUNK)


def place_kernel(width):
    def kernel(plan_ref, row_ref, a_ref, b_ref, s_ref, t_ref, out_ref, dq_ref, dk_ref, dv_ref,
               rows_buf, dq_buf, dk_buf, dv_buf, sems):
        here = lax.axis_index("ctx")
        side = lax.axis_index("head")
        z = here // 2
        source_a = up_down(z, side)
        plan = scalars(plan_ref, 2)
        half = dk_buf.shape[1]
        copies = []

        def send(buf, out, number):
            copy = pltpu.make_async_copy(buf, out, sems.at[number])
            copy.start()
            copies.append(copy)

        dk_buf[...] = s_ref[:, :half] + t_ref[:, :half]
        send(dk_buf, dk_ref, 0)
        dv_buf[...] = s_ref[:, half:] + t_ref[:, half:]
        send(dv_buf, dv_ref, 1)
        for slot in range(2):
            wanted = plan[slot]
            to = pl.ds(slot * CHUNK, CHUNK)
            inside = row_of(wanted, here % 2)

            def put(rows):
                rows_buf[to, :] = rows[:, :width]
                dq_buf[to, :] = rows[:, width:].astype(jnp.float32)

            home = wanted // 4 == z
            from_a = wanted // 4 == source_a
            pl.when(home)(lambda: put(row_ref[inside, :]))
            pl.when(from_a)(lambda: put(a_ref[to, :]))
            pl.when(jnp.logical_not(home | from_a))(lambda: put(b_ref[to, :]))
            send(rows_buf.at[to, :], out_ref.at[to, :], 2 + 2 * slot)
            send(dq_buf.at[to, :], dq_ref.at[to, :], 3 + 2 * slot)
        for copy in copies:
            copy.wait()

    return kernel


def per_device(queries, key_input, value_input, grad_out, doc_lengths, stretch_plan):
    tok, head_dim = key_input.shape
    width = queries.shape[1]
    heads = width // head_dim
    n = lax.axis_size("ctx")
    rounds = (min(DOC_CAP, tok * n // 4) // tok + 1) // 2
    reach = 2 * rounds
    bf16, f32 = jnp.bfloat16, jnp.float32
    both = ("ctx", "head")
    cross = [(0, 1), (1, 0)]
    side = lax.axis_index("head")

    here = lax.axis_index("ctx")
    order = jnp.arange(doc_lengths.shape[0], dtype=jnp.int32)
    bounds = jnp.sum(jnp.where(order[None, :] <= order[:, None], doc_lengths[None, :], 0), axis=1)

    def begins(device):
        places = device * tok + jnp.arange(tok, dtype=jnp.int32)
        starts = jnp.max(jnp.where(bounds[:, None] <= places[None, :], bounds[:, None], 0), axis=0)
        starts = starts.reshape(tok // CHUNK, 1, CHUNK)
        return jnp.broadcast_to(starts, (tok // CHUNK, heads, CHUNK)).reshape(tok // CHUNK, -1)

    def lanes_of(values):
        return jnp.pad(values, (0, 128 - values.shape[0])).reshape(1, 128)

    def fetch_pairs(r):
        pairs = []
        for s in range(n):
            for h in range(2):
                to = s // 2 + r + 1
                column = (s + h) % 2 if to < n // 2 else s % 2
                pairs.append((2 * s + h, 2 * (2 * (to % (n // 2)) + column) + h))
        return pairs

    def back_pairs(r):
        return [(s, s - 2 * r) for s in range(2 * r, n)]

    plan_out, own_kv, half, queries_grads = pl.pallas_call(
        pack_kernel,
        out_shape=(
            pltpu.VMEM(stretch_plan.shape, jnp.int32),
            pltpu.VMEM((tok, 2 * head_dim), bf16),
            pltpu.VMEM((tok, head_dim), bf16),
            pltpu.VMEM((tok, 2 * width), bf16),
        ),
        in_specs=[pl.BlockSpec(memory_space=pl.ANY)] * 5,
        out_specs=(VMEM,) * 4,
        scratch_shapes=[pltpu.SemaphoreType.DMA((5,))],
        name="pack",
    )(stretch_plan, key_input, value_input, queries, grad_out)
    tie_a, tie_b = row_pairs(n // 2)
    near = [(i, i ^ 1) for i in range(n)]
    part = lax.ppermute(queries_grads, "ctx", near)
    half_next = lax.ppermute(half, "ctx", near)
    mine = [lax.ppermute(own_kv, both, fetch_pairs(r)) for r in range(rounds)]
    mine = jnp.stack(mine)
    other = lax.ppermute(mine, "head", cross)
    half_cross = lax.ppermute(half_next, "head", cross)
    sizes = (rounds, reach, tok, heads, head_dim)
    params = pltpu.CompilerParams(vmem_limit_bytes=40 << 20)
    span = 2 * reach + 2
    weights = pltpu.VMEM((span * CHUNK, 2 * heads * CHUNK), bf16)
    scores = pltpu.VMEM((2, span, CHUNK, heads * CHUNK), f32)
    buffer = jax.ShapeDtypeStruct(((2 * rounds + 2) * tok, head_dim), bf16)
    rows = jax.ShapeDtypeStruct((tok, 2 * width), bf16)
    attended = jax.ShapeDtypeStruct((2 * head_dim, heads * CHUNK), bf16)
    grads = jax.ShapeDtypeStruct((span * CHUNK, 2 * heads * CHUNK), bf16)
    key_sums = jax.ShapeDtypeStruct((rounds + 1, tok, 2 * head_dim), f32)
    att_own, d_own, kv_own, kbuf, vbuf = pl.pallas_call(
        own_kernel(sizes),
        out_shape=(attended, grads, key_sums, buffer, buffer),
        in_specs=[VMEM] * 9,
        out_specs=(VMEM,) * 5,
        scratch_shapes=[scores, weights],
        compiler_params=params,
        name="attend_own",
    )(begins(here), key_input, value_input, queries, grad_out, mine, other, half_next,
      half_cross)
    kv_own, stretch_here = lax.optimization_barrier((kv_own, plan_out))
    plan_mine = lax.ppermute(stretch_here, both, tie_a)
    plan_other = lax.ppermute(plan_mine, "head", cross)
    plans = jnp.where(side == 0, jnp.concatenate([plan_mine, plan_other]),
                      jnp.concatenate([plan_other, plan_mine]))
    att_next, d_next, kv_sum, far = pl.pallas_call(
        next_kernel(sizes),
        out_shape=(
            attended, grads, jax.ShapeDtypeStruct((tok, 2 * head_dim), f32),
            jax.ShapeDtypeStruct((rounds, tok, 2 * head_dim), bf16),
        ),
        in_specs=[VMEM] * 5,
        out_specs=(VMEM,) * 4,
        scratch_shapes=[scores, weights, pltpu.VMEM((rounds, tok, 2 * head_dim), f32)],
        compiler_params=params,
        name="attend_next",
    )(begins(here ^ 1), kbuf, vbuf, part, kv_own)
    od, send_a, send_b = pl.pallas_call(
        send_kernel(sizes),
        out_shape=(jax.ShapeDtypeStruct((2 * tok, 2 * width), bf16), rows, rows),
        in_specs=[VMEM] * 6,
        out_specs=(VMEM,) * 3,
        compiler_params=params,
        name="send_rows",
    )(lanes_of(plans), kbuf, d_own, d_next, att_own, att_next)

    moved_a = lax.ppermute(send_a, both, tie_a)
    moved_b = lax.ppermute(send_b, both, tie_b)
    total = kv_sum
    for r in range(rounds):
        total = total + lax.ppermute(far[r], "ctx", back_pairs(r + 1)).astype(f32)
    total_other = lax.ppermute(total, "head", cross)

    output, query_grad, key_grad, value_grad = pl.pallas_call(
        place_kernel(width),
        out_shape=(
            jax.ShapeDtypeStruct((tok, width), bf16),
            jax.ShapeDtypeStruct((tok, width), f32),
            jax.ShapeDtypeStruct((tok, head_dim), f32),
            jax.ShapeDtypeStruct((tok, head_dim), f32),
        ),
        in_specs=[VMEM] * 6,
        out_specs=(pl.BlockSpec(memory_space=pl.ANY),) * 4,
        scratch_shapes=[
            pltpu.VMEM((tok, width), bf16), pltpu.VMEM((tok, width), f32),
            pltpu.VMEM((tok, head_dim), f32), pltpu.VMEM((tok, head_dim), f32),
            pltpu.SemaphoreType.DMA((6,)),
        ],
        compiler_params=pltpu.CompilerParams(vmem_limit_bytes=32 << 20),
        name="place",
    )(lanes_of(stretch_plan), od, moved_a, moved_b, total, total_other)
    return (output, query_grad, key_grad, value_grad)


def solution(mesh):
    return jax.shard_map(
        per_device,
        mesh=mesh,
        in_specs=(
            P(("groups", "ctx"), "head"),
            P(("groups", "ctx"), None),
            P(("groups", "ctx"), None),
            P(("groups", "ctx"), "head"),
            P("groups"),
            P(("groups", "ctx")),
        ),
        out_specs=(
            P(("groups", "ctx"), "head"),
            P(("groups", "ctx"), "head"),
            P(("groups", "ctx"), None),
            P(("groups", "ctx"), None),
        ),
        check_vma=False,
    )
```
